32 devices in a mesh: tm: 8 (over y, x, core), vocab: 4 (over z).
Axes of the slice: x: 2, y: 2, z: 4, core: 2. Of those that a mesh axis runs over, the one named last changes fastest.
Arguments:
- drift_noise: bfloat16 [64, 128, 8192], P('tm', None, 'vocab'), may hold values from -6 to 6
- counts: bfloat16 [64, 128, 8192], P('tm', None, 'vocab'), may hold values from 0 to 12, as said below
- base_logits: float32 [128, 8192], P(None, 'vocab'), may hold values from -8 to 300
- drift_scale: float32 [128], replicated, may hold values from 0.05 to 0.5
Outputs:
- grad_noise: bfloat16 [64, 128, 8192], P('tm', None, 'vocab')
- grad_base: float32 [128, 8192], P('tm', 'vocab')
The draws below stay inside these ranges and needn't reach their ends.
Inputs may be any that keep to these rules, and one draw needn't show every extreme that they name: `counts`: whole numbers.
All inputs are finite; a program needn't handle non-finite values.
Results may differ from the reference program's by a relative error of at most 0.003.
Values sent between devices are 32-bit elements; how exact they have to be, the bound alone decides.
A program may use at most 128 MiB of HBM per device.

```python
import math
import jax
import jax.numpy as jnp
from jax import lax

TOPICS = 128
VOCAB = 8192
SLICES = 64


def draw_counts(key, part):
    column = jnp.arange(VOCAB, dtype=jnp.int32)
    highest = 12 - 10 * column // VOCAB
    raw = jax.random.randint(key, (SLICES, TOPICS, VOCAB), 0, 1 << 20, dtype=jnp.int32)
    values = raw % (highest + 1)
    return values.astype(jnp.float32).astype(jnp.bfloat16)


def draw_base_logits(key, part):
    column = jnp.arange(VOCAB, dtype=jnp.int32)
    trend = 1.5 - 3.0 * column.astype(jnp.float32) / VOCAB
    rough = jax.random.normal(key, (TOPICS, VOCAB), jnp.float32)
    return jnp.clip(rough, -6.0, 6.0) + trend[None, :]


def steps_of(own_key, extent, split, smallest, top_value):
    loudness = 1.0
    for dim, blocks in split:
        heights = jax.random.uniform(jax.random.fold_in(jax.random.fold_in(own_key, 6), dim), (blocks,), jnp.float32, smallest / len(split), top_value / len(split))
        loudness = loudness * jnp.repeat(jnp.exp(heights), extent[dim] // blocks).reshape((-1,) + (1,) * (len(extent) - 1 - dim))
    return loudness


def scatter_about(key, shape, width, most, cuts=(), kind=jnp.bfloat16):
    entries = jax.random.normal(key, shape, jnp.float32) * width
    if len(cuts) > 0:
        entries = steps_of(key, shape, cuts, -0.22, 0.18) * entries
    return jnp.clip(entries, min=-most, max=most).astype(kind)


def setup_inputs(seed: int = 0) -> dict:
    streams_of = jax.random.split(jax.random.key(seed), 5)
    drift_noise = scatter_about(streams_of[0], (SLICES, TOPICS, VOCAB), 1.0, 6.0, ((0, 8), (2, 4)))
    counts = draw_counts(jax.random.fold_in(streams_of[4], 71), 0)
    base_logits = draw_base_logits(jax.random.fold_in(streams_of[4], 71), 0)
    drift_scale = jnp.clip(jnp.exp(jax.random.uniform(streams_of[3], (TOPICS,), jnp.float32, math.log(0.05), math.log(0.5))), 0.05, 0.5)
    return dict(drift_noise=drift_noise, counts=counts, base_logits=base_logits, drift_scale=drift_scale)


def reference(drift_noise, counts, base_logits, drift_scale):
    spread = drift_scale[:, None]

    def forward(carry, inputs):
        noise, count_row = inputs
        carry = carry + spread * noise.astype(jnp.float32)
        logits = base_logits + carry
        top = jnp.max(logits, axis=1, keepdims=True)
        expo = jnp.exp(logits - top)
        total = jnp.sum(expo, axis=1, keepdims=True)
        count_f = count_row.astype(jnp.float32)
        tokens = jnp.sum(count_f, axis=1, keepdims=True)
        slope = count_f - tokens * (expo / total)
        return carry, slope

    start = jnp.zeros(base_logits.shape, jnp.float32)
    _, slopes = lax.scan(forward, start, (drift_noise, counts))

    def backward(carry, slope):
        carry = carry + slope
        return carry, carry

    whole, suffix = lax.scan(backward, start, slopes, reverse=True)
    grad_noise = (spread[None] * suffix - drift_noise.astype(jnp.float32)).astype(jnp.bfloat16)
    return grad_noise, whole
```

```python
import functools

import jax
import jax.numpy as jnp
from jax import lax
from jax.experimental import pallas as pl
from jax.experimental.pallas import tpu as pltpu
from jax.sharding import PartitionSpec as P

MESH = pl.DeviceIdType.MESH
KC = 16
HB = KC // 2
LANE = 128
FORWARD = (3,3,1,4)
REVERSE = (1,4,4,2)
EARLY = 2


def kernel(n, nz, nb, rows, out_rows, dims,
           noise_hbm, counts_hbm, base_hbm, scale_hbm, gn_hbm, gb_hbm,
           noise, counts, base, scale_ref, spread, work, whole, ratio, known, stat, stat_in, tot, tot_out,
           own, mate, src, got, part, share, enter,
           in_sem, out_sem, gb_sem, scale_sem, mate_s, mate_r, hop_s, hop_r, acc_s, acc_r, stat_s, stat_r, tot_s, tot_r):
    T, K, V = dims
    NC = K // KC
    LB = min(256, V)
    VH = V // 2
    per = KC // rows
    me = lax.axis_index("tm")
    z = lax.axis_index("vocab")
    core = lax.rem(me, 2)
    partner = me + 1 - 2 * core
    chip = me // 2

    def bit(j):
        return lax.rem(chip // (2 ** j), 2)

    def across(j):
        return me + (1 - 2 * bit(j)) * (2 ** (j + 1))

    def order(a, j):
        return j if a == 0 else nb - 1 - j

    def upper(p, b):
        return bit(b) == 1 - p

    def above(p, b):
        high = chip // (2 ** (b + 1))
        return high != (0 if p == 0 else 2 ** (nb - 1 - b) - 1)

    def always(x):
        return isinstance(x, bool)

    def sends(p, a, j):
        b = order(a, j)
        if a == 0:
            return True if j < nb - 1 else jnp.logical_not(upper(p, b))
        low = jnp.logical_not(upper(p, b))
        return low if j == 0 else jnp.logical_or(low, above(p, b))

    def receives(p, a, j):
        b = order(a, j)
        if a == 0:
            return True if j < nb - 1 else upper(p, b)
        return upper(p, b) if j == 0 else jnp.logical_or(upper(p, b), above(p, b))

    def guarded(cond, fn):
        if always(cond):
            fn()
        else:
            pl.when(cond)(fn)

    def half(a):
        return pl.ds(a * VH, VH)

    def krows(c):
        return pl.ds(pl.multiple_of(c * KC, KC), KC)

    def load_noise(c):
        return pltpu.make_async_copy(noise_hbm.at[:, krows(c), :], noise.at[c], in_sem.at[0, c])

    def load_counts(c):
        return pltpu.make_async_copy(counts_hbm.at[:, krows(c), :], counts.at[c], in_sem.at[1, c])

    def load_base(c):
        return pltpu.make_async_copy(base_hbm.at[krows(c), :], base.at[c], in_sem.at[2, c])

    def store_out(c):
        return pltpu.make_async_copy(noise.at[c], gn_hbm.at[:, krows(c), :], out_sem.at[c])

    def send(a, b, s, r, device):
        return pltpu.make_async_remote_copy(src_ref=a, dst_ref=b, send_sem=s, recv_sem=r,
                                            device_id=device, device_id_type=MESH)

    def mate_copy(p, c):
        return send(own.at[p, c, 1 - core], mate.at[p, c], mate_s.at[p, c], mate_r.at[p, c], {"tm": partner})

    def hop_copy(p, a, j, c):
        return send(src.at[p, j, c, :, half(a)], got.at[p, j, c, :, half(a)],
                    hop_s.at[p, a, j, c], hop_r.at[p, a, j, c], {"tm": across(order(a, j))})

    def share_copy(p, c):
        return send(share.at[p, c], enter.at[p, c, core], acc_s.at[p, c], acc_r.at[p, c], {"tm": partner})

    def stat_copy(d, c):
        return send(stat.at[c], stat_in.at[d - 1, c], stat_s.at[d - 1, c], stat_r.at[d - 1, c],
                    {"vocab": lax.rem(z + d, nz)})

    def slot():
        return core if per == 1 else 0

    def owner(c, e):
        return c * per + e

    def tot_copy(c, e):
        return send(tot_out.at[c], tot.at[slot()], tot_s.at[c, e], tot_r.at[slot()], {"tm": owner(c, e)})

    def holds(e):
        return chip == 0 if per == 1 else me == (e * rows) // HB

    def each(fn):
        lax.fori_loop(0, NC, lambda i, _: (fn(NC - 1 - i), 0)[1], 0)

    load_scale = pltpu.make_async_copy(scale_hbm, scale_ref, scale_sem.at[0])
    load_scale.start()
    each(lambda c: load_noise(c).start())
    each(lambda c: load_counts(c).start())
    each(lambda c: load_base(c).start())

    barrier = pltpu.get_barrier_semaphore()
    pl.semaphore_signal(barrier, inc=1, device_id={"tm": partner}, device_id_type=MESH)
    for j in range(nb):
        pl.semaphore_signal(barrier, inc=1, device_id={"tm": across(j)}, device_id_type=MESH)
    for d in range(1, nz):
        pl.semaphore_signal(barrier, inc=1, device_id={"vocab": lax.rem(z + d, nz)}, device_id_type=MESH)
    for h in range(2):
        @pl.when(me != h)
        def _():
            pl.semaphore_signal(barrier, inc=1, device_id={"tm": h}, device_id_type=MESH)

    load_scale.wait()
    wide = jnp.broadcast_to(scale_ref[...], (LANE, LANE)).T
    for c in range(NC):
        spread[c] = wide[c * KC:(c + 1) * KC]

    def lanes(i):
        return pl.ds(pl.multiple_of(i * LB, LB), LB)

    def tiled(x):
        return jnp.concatenate([x] * (LB // LANE), axis=1)

    def two(x):
        return x.reshape(2, HB, x.shape[-1])

    def narrow(sums, e):
        for b in range(LB // LANE):
            sums = sums + e[:, b * LANE:(b + 1) * LANE]
        return sums

    def local(c):
        load_noise(c).wait()
        sp = tiled(spread[c])

        def block(i, _):
            total = jnp.zeros((KC, LB), jnp.float32)
            for t in range(T):
                total = total + noise[c, t, :, lanes(i)].astype(jnp.float32)
            own[0, c, :, :, lanes(i)] = two(sp * total)
            return 0

        lax.fori_loop(0, V // LB, block, 0)

    def expand(c):
        load_counts(c).wait()
        sp = tiled(spread[c])

        def block(i, sums):
            total = jnp.zeros((KC, LB), jnp.float32)
            seen = jnp.zeros((KC, LB), jnp.float32)
            new = []
            for t in range(T):
                total = total + noise[c, t, :, lanes(i)].astype(jnp.float32)
                work[c, t, :, lanes(i)] = jnp.exp(sp * total)
                count = counts[c, t, :, lanes(i)].astype(jnp.float32)
                seen = seen + count
                new.append(narrow(sums[t], count))
            whole[c, :, lanes(i)] = seen
            return tuple(new)

        sums = lax.fori_loop(0, V // LB, block, tuple(jnp.zeros((KC, LANE), jnp.float32) for _ in range(T)))
        lane = lax.broadcasted_iota(jnp.int32, (KC, LANE), 1)
        packed = jnp.zeros((KC, LANE), jnp.float32)
        for t in range(T):
            packed = jnp.where(lane == T + t, jnp.sum(sums[t], axis=1, keepdims=True), packed)
        known[c] = packed

    def start_hops(p, j, c):
        for a in ((0, 1) if (j + p) % 2 == 0 else (1, 0)):
            guarded(sends(p, a, j), lambda a=a: hop_copy(p, a, j, c).start())

    def first(p, c):
        mate_copy(p, c).wait_recv()
        src[p, 0, c] = own[p, c, core] + mate[p, c]
        part[p, c] = jnp.zeros((HB, V), jnp.float32)
        start_hops(p, 0, c)

    def hop(p, j, c):
        for a in range(2):
            up = upper(p, order(a, j))

            def take(a=a, up=up):
                hop_copy(p, a, j, c).wait_recv()
                arrived = got[p, j, c, :, half(a)]
                if a == 0:
                    if j < nb - 1:
                        src[p, j + 1, c, :, half(a)] = src[p, j, c, :, half(a)] + arrived
                        arrived = jnp.where(up, arrived, jnp.zeros_like(arrived))
                part[p, c, :, half(a)] = part[p, c, :, half(a)] + arrived

            guarded(receives(p, a, j), take)
        if j < nb - 1:
            low = jnp.logical_not(upper(p, order(1, j + 1)))
            chips = src[p, 0, c, :, half(1)]
            src[p, j + 1, c, :, half(1)] = part[p, c, :, half(1)] + jnp.where(low, chips, jnp.zeros_like(chips))
            start_hops(p, j + 1, c)
            return
        before = part[p, c]
        leads = core == p
        mine, other = own[p, c, core], mate[p, c]
        zero = jnp.zeros_like(before)
        share[p, c] = before + jnp.where(leads, mine, zero)
        enter[p, c, core] = before + jnp.where(leads, zero, other)
        share_copy(p, c).start()
        if p == 1:
            @pl.when(chip == 0)
            def _():
                tot_out[c] = before + src[1, 0, c]
                for e in range(per):
                    @pl.when(holds(e) & (owner(c, e) != me))
                    def _():
                        tot_copy(c, e).start()

                    @pl.when(holds(e) & (owner(c, e) == me))
                    def _():
                        tot[slot()] = tot_out[c]

    def soft(c):
        share_copy(0, c).wait_recv()
        load_base(c).wait()

        def seek(i, top):
            q = base[c, :, lanes(i)] + enter[0, c, :, :, lanes(i)].reshape(KC, LB)
            base[c, :, lanes(i)] = q
            for b in range(LB // LANE):
                top = jnp.maximum(top, q[:, b * LANE:(b + 1) * LANE])
            return top

        top = lax.fori_loop(0, V // LB, seek, jnp.full((KC, LANE), -jnp.inf, jnp.float32))
        top = jnp.broadcast_to(jnp.max(top, axis=1, keepdims=True), (KC, LANE))
        tops = tiled(top)

        def block(i, sums):
            w = jnp.exp(base[c, :, lanes(i)] - tops)
            base[c, :, lanes(i)] = w
            return tuple(narrow(sums[t], w * work[c, t, :, lanes(i)]) for t in range(T))

        sums = lax.fori_loop(0, V // LB, block, tuple(jnp.zeros((KC, LANE), jnp.float32) for _ in range(T)))
        lane = lax.broadcasted_iota(jnp.int32, (KC, LANE), 1)
        packed = jnp.where(lane < 2 * T, known[c], top)
        for t in range(T):
            packed = jnp.where(lane == t, jnp.sum(sums[t], axis=1, keepdims=True), packed)
        stat[c] = jnp.where(lane[:HB] < LANE // 2, packed[:HB], pltpu.roll(packed[HB:], LANE // 2, 1))
        for d in range(1, nz):
            stat_copy(d, c).start()

    def slopes(c):
        for d in range(1, nz):
            stat_copy(d, c).wait_recv()
        seen = [stat[c]] + [stat_in[d - 1, c] for d in range(1, nz)]
        tops = [pltpu.roll(x, LANE - 2 * T, 1) for x in seen]
        best, tokens = tops[0], seen[0]
        for d in range(1, nz):
            best = jnp.maximum(best, tops[d])
            tokens = tokens + seen[d]
        factor = [jnp.exp(top - best) for top in tops]
        total = factor[0] * seen[0]
        for d in range(1, nz):
            total = total + factor[d] * seen[d]
        r = factor[0] * pltpu.roll(tokens, LANE - T, 1) / total
        for t in range(T):
            for h in range(2):
                k = h * (LANE // 2) + t
                ratio[c, t, h * HB:(h + 1) * HB] = jnp.broadcast_to(r[:, k:k + 1], (HB, LANE))

        def block(i, _):
            drawn = jnp.zeros((KC, LB), jnp.float32)
            for t in range(T):
                drawn = drawn + tiled(ratio[c, t]) * work[c, t, :, lanes(i)]
            own[1, c, :, :, lanes(i)] = two(whole[c, :, lanes(i)] - base[c, :, lanes(i)] * drawn)
            return 0

        lax.fori_loop(0, V // LB, block, 0)
        mate_copy(1, c).start()

    def finish(c):
        share_copy(1, c).wait_recv()
        sp = tiled(spread[c])

        def block(i, _):
            w = base[c, :, lanes(i)]
            run = enter[1, c, :, :, lanes(i)].reshape(KC, LB)
            drawn = jnp.zeros((KC, LB), jnp.float32)
            for t in reversed(range(T)):
                drawn = drawn + tiled(ratio[c, t]) * work[c, t, :, lanes(i)]
                run = run + counts[c, t, :, lanes(i)].astype(jnp.float32)
                value = sp * (run - w * drawn) - noise[c, t, :, lanes(i)].astype(jnp.float32)
                noise[c, t, :, lanes(i)] = value.astype(jnp.bfloat16)
            return 0

        lax.fori_loop(0, V // LB, block, 0)
        store_out(c).start()

    each(local)
    for i in range(EARLY):
        expand(NC - 1 - i)
    pl.semaphore_wait(barrier, nb + nz + jnp.where(chip == 0, n - 1, 0))
    each(lambda c: mate_copy(0, c).start())

    at, plan = 0, [(0, functools.partial(first, 0))]
    for j in range(nb):
        at += FORWARD[0 if j == 0 else 1]
        plan.append((at, functools.partial(hop, 0, j)))
    at += FORWARD[2]
    plan.append((at, soft))
    at += FORWARD[3]
    plan.append((at, slopes))
    at += REVERSE[0]
    plan.append((at, functools.partial(first, 1)))
    for j in range(nb):
        at += REVERSE[1 if j == 0 else 2]
        plan.append((at, functools.partial(hop, 1, j)))
    at += REVERSE[3]
    plan.append((at, finish))
    plan = plan[::-1]

    def tick(s, _):
        for off, stage in plan:
            @pl.when((s >= off) & (s < off + NC))
            def _():
                stage(NC - 1 - (s - off))

        @pl.when(s < NC - EARLY)
        def _():
            expand(NC - 1 - EARLY - s)
        return 0

    lax.fori_loop(0, NC + at, tick, 0)

    begin = me * rows - ((me * rows) // KC) * KC
    if per == 1:
        for h in range(2):
            @pl.when(me != h)
            def _():
                send(tot_out.at[0], tot.at[h], tot_s.at[0, 0], tot_r.at[h], {"tm": h}).wait_recv()
    else:
        @pl.when(me != begin // HB)
        def _():
            send(tot_out.at[0], tot.at[0], tot_s.at[0, 0], tot_r.at[0], {"tm": 0}).wait_recv()
    if per == 1:
        done = [pltpu.make_async_copy(tot.at[h], gb_hbm.at[pl.ds(h * HB, HB), :], gb_sem.at[h]) for h in range(2)]
    else:
        done = [pltpu.make_async_copy(tot.at[0], gb_hbm, gb_sem.at[0])]
    for copy in done:
        copy.start()

    def drain(c):
        for p in (0, 1):
            mate_copy(p, c).wait_send()
            for a in range(2):
                for j in range(nb):
                    guarded(sends(p, a, j), lambda p=p, a=a, j=j: hop_copy(p, a, j, c).wait_send())
            share_copy(p, c).wait_send()
        for d in range(1, nz):
            stat_copy(d, c).wait_send()
        for e in range(per):
            @pl.when((chip == 0) & holds(e) & (owner(c, e) != me))
            def _():
                tot_copy(c, e).wait_send()
        store_out(c).wait()

    each(drain)
    for copy in done:
        copy.wait()


def per_device(n, nz, drift_noise, counts, base_logits, drift_scale):
    T, K, V = drift_noise.shape
    nb = n.bit_length() - 2
    rows = K // n
    out_rows = KC if rows >= KC else HB
    NC = K // KC
    f32, bf16 = jnp.float32, jnp.bfloat16
    dma = pltpu.SemaphoreType.DMA
    any_space = pl.BlockSpec(memory_space=pl.ANY)
    peers = max(nz - 1, 1)
    grad_noise, grad_base = pl.pallas_call(
        functools.partial(kernel, n, nz, nb, rows, out_rows, (T, K, V)),
        out_shape=(jax.ShapeDtypeStruct((T, K, V), bf16), jax.ShapeDtypeStruct((out_rows, V), f32)),
        in_specs=[any_space] * 4,
        out_specs=(any_space, any_space),
        scratch_shapes=[
            pltpu.VMEM((NC, T, KC, V), bf16),
            pltpu.VMEM((NC, T, KC, V), bf16),
            pltpu.VMEM((NC, KC, V), f32),
            pltpu.VMEM((1, K), f32),
            pltpu.VMEM((NC, KC, LANE), f32),
            pltpu.VMEM((NC, T, KC, V), f32),
            pltpu.VMEM((NC, KC, V), f32),
            pltpu.VMEM((NC, T, KC, LANE), f32),
            pltpu.VMEM((NC, KC, LANE), f32),
            pltpu.VMEM((NC, HB, LANE), f32),
            pltpu.VMEM((peers, NC, HB, LANE), f32),
            pltpu.VMEM((2, HB, V), f32),
            pltpu.VMEM((NC, HB, V), f32),
            pltpu.VMEM((2, NC, 2, HB, V), f32),
            pltpu.VMEM((2, NC, HB, V), f32),
            pltpu.VMEM((2, nb, NC, HB, V), f32),
            pltpu.VMEM((2, nb, NC, HB, V), f32),
            pltpu.VMEM((2, NC, HB, V), f32),
            pltpu.VMEM((2, NC, HB, V), f32),
            pltpu.VMEM((2, NC, 2, HB, V), f32),
            dma((3, NC)), dma((NC,)), dma((2,)), dma((1,)),
            dma((2, NC)), dma((2, NC)),
            dma((2, 2, nb, NC)), dma((2, 2, nb, NC)),
            dma((2, NC)), dma((2, NC)),
            dma((peers, NC)), dma((peers, NC)),
            dma((NC, KC // rows)), dma((2,)),
        ],
        compiler_params=pltpu.CompilerParams(
            collective_id=0, has_side_effects=True, vmem_limit_bytes=46 * 1024 * 1024),
    )(*[pltpu.with_memory_space_constraint(x, pltpu.HBM) for x in (drift_noise, counts, base_logits, drift_scale.reshape(1, K))])
    if rows < out_rows:
        start = lax.rem(lax.axis_index("tm") * rows, out_rows)
        grad_base = lax.dynamic_slice_in_dim(grad_base, start, rows, 0)
    return grad_noise, grad_base


def solution(mesh):
    n, nz = mesh.shape["tm"], mesh.shape["vocab"]
    return jax.shard_map(
        functools.partial(per_device, n, nz),
        mesh=mesh,
        in_specs=(P("tm", None, "vocab"), P("tm", None, "vocab"), P(None, "vocab"), P()),
        out_specs=(P("tm", None, "vocab"), P("tm", "vocab")),
        check_vma=False,
    )
```

```python
import functools

import jax
import jax.numpy as jnp
from jax import lax
from jax.experimental import pallas as pl
from jax.experimental.pallas import tpu as pltpu
from jax.sharding import PartitionSpec as P

MESH = pl.DeviceIdType.MESH
KC = 16
HB = KC // 2
LANE = 128
FORWARD = (3,3,1,4)
REVERSE = (1,4,4,2)
EARLY = 3
ORDER = [(10, 3), (0, 0), (10, 4), (0, 1), (10, 5), (0, 2), (10, 6), (0, 3), (10, 7), (9, 0), (9, 1), (1, 0), (9, 2), (1, 1), (9, 3), (0, 4), (1, 2), (9, 4), (0, 5), (2, 0), (1, 3), (9, 5), (0, 6), (3, 0), (2, 1), (1, 4), (9, 6), (0, 7), (3, 1), (2, 2), (1, 5), (9, 7), (3, 2), (2, 3), (1, 6), (3, 3), (2, 4), (1, 7), (4, 0), (3, 4), (2, 5), (5, 0), (4, 1), (3, 5), (2, 6), (5, 1), (4, 2), (3, 6), (2, 7), (5, 2), (4, 3), (3, 7), (5, 3), (4, 4), (6, 0), (5, 4), (4, 5), (6, 1), (5, 5), (4, 6), (6, 2), (5, 6), (4, 7), (6, 3), (5, 7), (7, 0), (6, 4), (7, 1), (6, 5), (8, 0), (7, 2), (6, 6), (8, 1), (7, 3), (6, 7), (8, 2), (7, 4), (8, 3), (7, 5), (8, 4), (7, 6), (8, 5), (7, 7), (8, 6), (8, 7)]


def kernel(n, nz, nb, rows, out_rows, dims,
           noise_hbm, counts_hbm, base_hbm, scale_hbm, gn_hbm, gb_hbm,
           noise, counts, base, scale_ref, spread, work, whole, ratio, known, stat, stat_in, tot, tot_out,
           own, mate, src, got, part, share, enter,
           in_sem, out_sem, gb_sem, scale_sem, mate_s, mate_r, hop_s, hop_r, acc_s, acc_r, stat_s, stat_r, tot_s, tot_r):
    T, K, V = dims
    NC = K // KC
    LB = min(256, V)
    VH = V // 2
    per = KC // rows
    me = lax.axis_index("tm")
    z = lax.axis_index("vocab")
    core = lax.rem(me, 2)
    partner = me + 1 - 2 * core
    chip = me // 2

    def bit(j):
        return lax.rem(chip // (2 ** j), 2)

    def across(j):
        return me + (1 - 2 * bit(j)) * (2 ** (j + 1))

    def order(a, j):
        return j if a == 0 else nb - 1 - j

    def upper(p, b):
        return bit(b) == 1 - p

    def above(p, b):
        high = chip // (2 ** (b + 1))
        return high != (0 if p == 0 else 2 ** (nb - 1 - b) - 1)

    def always(x):
        return isinstance(x, bool)

    def sends(p, a, j):
        b = order(a, j)
        if a == 0:
            return True if j < nb - 1 else jnp.logical_not(upper(p, b))
        low = jnp.logical_not(upper(p, b))
        return low if j == 0 else jnp.logical_or(low, above(p, b))

    def receives(p, a, j):
        b = order(a, j)
        if a == 0:
            return True if j < nb - 1 else upper(p, b)
        return upper(p, b) if j == 0 else jnp.logical_or(upper(p, b), above(p, b))

    def guarded(cond, fn):
        if always(cond):
            fn()
        else:
            pl.when(cond)(fn)

    def half(a):
        return pl.ds(a * VH, VH)

    def krows(c):
        return pl.ds(pl.multiple_of(c * KC, KC), KC)

    def load_noise(c):
        return pltpu.make_async_copy(noise_hbm.at[:, krows(c), :], noise.at[c], in_sem.at[0, c])

    def load_counts(c):
        return pltpu.make_async_copy(counts_hbm.at[:, krows(c), :], counts.at[c], in_sem.at[1, c])

    def load_base(c):
        return pltpu.make_async_copy(base_hbm.at[krows(c), :], base.at[c], in_sem.at[2, c])

    def store_out(c):
        return pltpu.make_async_copy(noise.at[c], gn_hbm.at[c], out_sem.at[c])

    def send(a, b, s, r, device):
        return pltpu.make_async_remote_copy(src_ref=a, dst_ref=b, send_sem=s, recv_sem=r,
                                            device_id=device, device_id_type=MESH)

    def mate_copy(p, c):
        return send(own.at[p, c, 1 - core], mate.at[p, c], mate_s.at[p, c], mate_r.at[p, c], {"tm": partner})

    def hop_copy(p, a, j, c):
        return send(src.at[p, j, c, :, half(a)], got.at[p, j, c, :, half(a)],
                    hop_s.at[p, a, j, c], hop_r.at[p, a, j, c], {"tm": across(order(a, j))})

    def share_copy(p, c):
        return send(share.at[p, c], enter.at[p, c, core], acc_s.at[p, c], acc_r.at[p, c], {"tm": partner})

    def stat_copy(d, c):
        return send(stat.at[c], stat_in.at[d - 1, c], stat_s.at[d - 1, c], stat_r.at[d - 1, c],
                    {"vocab": lax.rem(z + d, nz)})

    def slot():
        return core if per == 1 else 0

    def owner(c, e):
        return c * per + e

    def tot_copy(c, e):
        return send(tot_out.at[c], tot.at[slot()], tot_s.at[c, e], tot_r.at[slot()], {"tm": owner(c, e)})

    def holds(e):
        return chip == 0 if per == 1 else me == (e * rows) // HB

    def each(fn):
        lax.fori_loop(0, NC, lambda i, _: (fn(NC - 1 - i), 0)[1], 0)

    load_scale = pltpu.make_async_copy(scale_hbm, scale_ref, scale_sem.at[0])
    load_scale.start()
    each(lambda c: load_noise(c).start())

    barrier = pltpu.get_barrier_semaphore()
    pl.semaphore_signal(barrier, inc=1, device_id={"tm": partner}, device_id_type=MESH)
    for j in range(nb):
        pl.semaphore_signal(barrier, inc=1, device_id={"tm": across(j)}, device_id_type=MESH)
    for d in range(1, nz):
        pl.semaphore_signal(barrier, inc=1, device_id={"vocab": lax.rem(z + d, nz)}, device_id_type=MESH)
    for h in range(2):
        @pl.when(me != h)
        def _():
            pl.semaphore_signal(barrier, inc=1, device_id={"tm": h}, device_id_type=MESH)

    load_scale.wait()
    wide = jnp.broadcast_to(scale_ref[...], (LANE, LANE)).T
    for c in range(NC):
        spread[c] = wide[c * KC:(c + 1) * KC]

    def lanes(i):
        return pl.ds(pl.multiple_of(i * LB, LB), LB)

    def tiled(x):
        return jnp.concatenate([x] * (LB // LANE), axis=1)

    def two(x):
        return x.reshape(2, HB, x.shape[-1])

    def narrow(sums, e):
        for b in range(LB // LANE):
            sums = sums + e[:, b * LANE:(b + 1) * LANE]
        return sums

    def local(c):
        load_noise(c).wait()
        sp = tiled(spread[c])

        def block(i, _):
            total = jnp.zeros((KC, LB), jnp.float32)
            for t in range(T):
                total = total + noise[c, t, :, lanes(i)].astype(jnp.float32)
            own[0, c, :, :, lanes(i)] = two(sp * total)
            return 0

        lax.fori_loop(0, V // LB, block, 0)

    def expand(c):
        load_counts(c).wait()
        sp = tiled(spread[c])

        def block(i, sums):
            total = jnp.zeros((KC, LB), jnp.float32)
            seen = jnp.zeros((KC, LB), jnp.float32)
            new = []
            for t in range(T):
                total = total + noise[c, t, :, lanes(i)].astype(jnp.float32)
                work[c, t, :, lanes(i)] = jnp.exp(sp * total)
                count = counts[c, t, :, lanes(i)].astype(jnp.float32)
                seen = seen + count
                new.append(narrow(sums[t], count))
            whole[c, :, lanes(i)] = seen
            return tuple(new)

        sums = lax.fori_loop(0, V // LB, block, tuple(jnp.zeros((KC, LANE), jnp.float32) for _ in range(T)))
        lane = lax.broadcasted_iota(jnp.int32, (KC, LANE), 1)
        packed = jnp.zeros((KC, LANE), jnp.float32)
        for t in range(T):
            packed = jnp.where(lane == T + t, jnp.sum(sums[t], axis=1, keepdims=True), packed)
        known[c] = packed

    def start_hops(p, j, c):
        for a in ((0, 1) if (j + p) % 2 == 0 else (1, 0)):
            guarded(sends(p, a, j), lambda a=a: hop_copy(p, a, j, c).start())

    def first(p, c):
        mate_copy(p, c).wait_recv()
        src[p, 0, c] = own[p, c, core] + mate[p, c]
        part[p, c] = jnp.zeros((HB, V), jnp.float32)
        start_hops(p, 0, c)

    def hop(p, j, c):
        for a in range(2):
            up = upper(p, order(a, j))

            def take(a=a, up=up):
                hop_copy(p, a, j, c).wait_recv()
                arrived = got[p, j, c, :, half(a)]
                if a == 0:
                    if j < nb - 1:
                        src[p, j + 1, c, :, half(a)] = src[p, j, c, :, half(a)] + arrived
                        arrived = jnp.where(up, arrived, jnp.zeros_like(arrived))
                part[p, c, :, half(a)] = part[p, c, :, half(a)] + arrived

            guarded(receives(p, a, j), take)
        if j < nb - 1:
            low = jnp.logical_not(upper(p, order(1, j + 1)))
            chips = src[p, 0, c, :, half(1)]
            src[p, j + 1, c, :, half(1)] = part[p, c, :, half(1)] + jnp.where(low, chips, jnp.zeros_like(chips))
            start_hops(p, j + 1, c)
            return
        before = part[p, c]
        leads = core == p
        mine, other = own[p, c, core], mate[p, c]
        zero = jnp.zeros_like(before)
        share[p, c] = before + jnp.where(leads, mine, zero)
        enter[p, c, core] = before + jnp.where(leads, zero, other)
        share_copy(p, c).start()
        if p == 1:
            @pl.when(chip == 0)
            def _():
                tot_out[c] = before + src[1, 0, c]
                for e in range(per):
                    @pl.when(holds(e) & (owner(c, e) != me))
                    def _():
                        tot_copy(c, e).start()

                    @pl.when(holds(e) & (owner(c, e) == me))
                    def _():
                        tot[slot()] = tot_out[c]

    def soft(c):
        share_copy(0, c).wait_recv()
        load_base(c).wait()

        def seek(i, top):
            q = base[c, :, lanes(i)] + enter[0, c, :, :, lanes(i)].reshape(KC, LB)
            base[c, :, lanes(i)] = q
            for b in range(LB // LANE):
                top = jnp.maximum(top, q[:, b * LANE:(b + 1) * LANE])
            return top

        top = lax.fori_loop(0, V // LB, seek, jnp.full((KC, LANE), -jnp.inf, jnp.float32))
        top = jnp.broadcast_to(jnp.max(top, axis=1, keepdims=True), (KC, LANE))
        tops = tiled(top)

        def block(i, sums):
            w = jnp.exp(base[c, :, lanes(i)] - tops)
            base[c, :, lanes(i)] = w
            return tuple(narrow(sums[t], w * work[c, t, :, lanes(i)]) for t in range(T))

        sums = lax.fori_loop(0, V // LB, block, tuple(jnp.zeros((KC, LANE), jnp.float32) for _ in range(T)))
        lane = lax.broadcasted_iota(jnp.int32, (KC, LANE), 1)
        packed = jnp.where(lane < 2 * T, known[c], top)
        for t in range(T):
            packed = jnp.where(lane == t, jnp.sum(sums[t], axis=1, keepdims=True), packed)
        stat[c] = jnp.where(lane[:HB] < LANE // 2, packed[:HB], pltpu.roll(packed[HB:], LANE // 2, 1))
        for d in range(1, nz):
            stat_copy(d, c).start()

    def slopes(c):
        for d in range(1, nz):
            stat_copy(d, c).wait_recv()
        seen = [stat[c]] + [stat_in[d - 1, c] for d in range(1, nz)]
        tops = [pltpu.roll(x, LANE - 2 * T, 1) for x in seen]
        best, tokens = tops[0], seen[0]
        for d in range(1, nz):
            best = jnp.maximum(best, tops[d])
            tokens = tokens + seen[d]
        factor = [jnp.exp(top - best) for top in tops]
        total = factor[0] * seen[0]
        for d in range(1, nz):
            total = total + factor[d] * seen[d]
        r = factor[0] * pltpu.roll(tokens, LANE - T, 1) / total
        for t in range(T):
            for h in range(2):
                k = h * (LANE // 2) + t
                ratio[c, t, h * HB:(h + 1) * HB] = jnp.broadcast_to(r[:, k:k + 1], (HB, LANE))

        def block(i, _):
            drawn = jnp.zeros((KC, LB), jnp.float32)
            for t in range(T):
                drawn = drawn + tiled(ratio[c, t]) * work[c, t, :, lanes(i)]
            own[1, c, :, :, lanes(i)] = two(whole[c, :, lanes(i)] - base[c, :, lanes(i)] * drawn)
            return 0

        lax.fori_loop(0, V // LB, block, 0)
        mate_copy(1, c).start()

    def finish(c):
        share_copy(1, c).wait_recv()
        sp = tiled(spread[c])

        def block(i, _):
            w = base[c, :, lanes(i)]
            run = enter[1, c, :, :, lanes(i)].reshape(KC, LB)
            drawn = jnp.zeros((KC, LB), jnp.float32)
            for t in reversed(range(T)):
                drawn = drawn + tiled(ratio[c, t]) * work[c, t, :, lanes(i)]
                run = run + counts[c, t, :, lanes(i)].astype(jnp.float32)
                value = sp * (run - w * drawn) - noise[c, t, :, lanes(i)].astype(jnp.float32)
                noise[c, t, :, lanes(i)] = value.astype(jnp.bfloat16)
            return 0

        lax.fori_loop(0, V // LB, block, 0)
        store_out(c).start()

    for k in range(EARLY):
        local(NC - 1 - k)
    each(lambda c: load_counts(c).start())
    each(lambda c: load_base(c).start())
    pl.semaphore_wait(barrier, nb + nz + jnp.where(chip == 0, n - 1, 0))
    for k in range(EARLY):
        mate_copy(0, NC - 1 - k).start()

    def opening(c):
        local(c)
        mate_copy(0, c).start()

    stages = [functools.partial(first, 0), functools.partial(hop, 0, 0), functools.partial(hop, 0, 1), soft, slopes,
              functools.partial(first, 1), functools.partial(hop, 1, 0), functools.partial(hop, 1, 1), finish, expand, opening]
    for st, k in ORDER:
        stages[st](NC - 1 - k)

    begin = me * rows - ((me * rows) // KC) * KC
    if per == 1:
        for h in range(2):
            @pl.when(me != h)
            def _():
                send(tot_out.at[0], tot.at[h], tot_s.at[0, 0], tot_r.at[h], {"tm": h}).wait_recv()
    else:
        @pl.when(me != begin // HB)
        def _():
            send(tot_out.at[0], tot.at[0], tot_s.at[0, 0], tot_r.at[0], {"tm": 0}).wait_recv()
    if per == 1:
        done = [pltpu.make_async_copy(tot.at[h], gb_hbm.at[pl.ds(h * HB, HB), :], gb_sem.at[h]) for h in range(2)]
    else:
        done = [pltpu.make_async_copy(tot.at[0], gb_hbm, gb_sem.at[0])]
    for copy in done:
        copy.start()

    def drain(c):
        for p in (0, 1):
            mate_copy(p, c).wait_send()
            for a in range(2):
                for j in range(nb):
                    guarded(sends(p, a, j), lambda p=p, a=a, j=j: hop_copy(p, a, j, c).wait_send())
            share_copy(p, c).wait_send()
        for d in range(1, nz):
            stat_copy(d, c).wait_send()
        for e in range(per):
            @pl.when((chip == 0) & holds(e) & (owner(c, e) != me))
            def _():
                tot_copy(c, e).wait_send()
        store_out(c).wait()

    each(drain)
    for copy in done:
        copy.wait()


def place(parts, base, gn_hbm, gb_hbm, sem):
    NC = parts.shape[0]
    copies = [pltpu.make_async_copy(parts.at[c], gn_hbm.at[:, pl.ds(c * KC, KC), :], sem.at[c]) for c in range(NC)]
    copies.append(pltpu.make_async_copy(base, gb_hbm, sem.at[NC]))
    for copy in copies:
        copy.start()
    for copy in copies:
        copy.wait()


def per_device(n, nz, drift_noise, counts, base_logits, drift_scale):
    T, K, V = drift_noise.shape
    nb = n.bit_length() - 2
    rows = K // n
    out_rows = KC if rows >= KC else HB
    NC = K // KC
    f32, bf16 = jnp.float32, jnp.bfloat16
    dma = pltpu.SemaphoreType.DMA
    any_space = pl.BlockSpec(memory_space=pl.ANY)
    peers = max(nz - 1, 1)
    parts, grad_base = pl.pallas_call(
        functools.partial(kernel, n, nz, nb, rows, out_rows, (T, K, V)),
        out_shape=(jax.ShapeDtypeStruct((NC, T, KC, V), bf16), jax.ShapeDtypeStruct((out_rows, V), f32)),
        in_specs=[any_space] * 4,
        out_specs=(any_space, any_space),
        scratch_shapes=[
            pltpu.VMEM((NC, T, KC, V), bf16),
            pltpu.VMEM((NC, T, KC, V), bf16),
            pltpu.VMEM((NC, KC, V), f32),
            pltpu.VMEM((1, K), f32),
            pltpu.VMEM((NC, KC, LANE), f32),
            pltpu.VMEM((NC, T, KC, V), f32),
            pltpu.VMEM((NC, KC, V), f32),
            pltpu.VMEM((NC, T, KC, LANE), f32),
            pltpu.VMEM((NC, KC, LANE), f32),
            pltpu.VMEM((NC, HB, LANE), f32),
            pltpu.VMEM((peers, NC, HB, LANE), f32),
            pltpu.VMEM((2, HB, V), f32),
            pltpu.VMEM((NC, HB, V), f32),
            pltpu.VMEM((2, NC, 2, HB, V), f32),
            pltpu.VMEM((2, NC, HB, V), f32),
            pltpu.VMEM((2, nb, NC, HB, V), f32),
            pltpu.VMEM((2, nb, NC, HB, V), f32),
            pltpu.VMEM((2, NC, HB, V), f32),
            pltpu.VMEM((2, NC, HB, V), f32),
            pltpu.VMEM((2, NC, 2, HB, V), f32),
            dma((3, NC)), dma((NC,)), dma((2,)), dma((1,)),
            dma((2, NC)), dma((2, NC)),
            dma((2, 2, nb, NC)), dma((2, 2, nb, NC)),
            dma((2, NC)), dma((2, NC)),
            dma((peers, NC)), dma((peers, NC)),
            dma((NC, KC // rows)), dma((2,)),
        ],
        compiler_params=pltpu.CompilerParams(
            collective_id=0, has_side_effects=True, vmem_limit_bytes=46 * 1024 * 1024),
    )(*[pltpu.with_memory_space_constraint(x, pltpu.HBM) for x in (drift_noise, counts, base_logits, drift_scale.reshape(1, K))])
    grad_noise, grad_base = pl.pallas_call(
        place,
        out_shape=(jax.ShapeDtypeStruct((T, K, V), bf16), jax.ShapeDtypeStruct((out_rows, V), f32)),
        in_specs=[any_space] * 2,
        out_specs=(any_space, any_space),
        scratch_shapes=[dma((NC + 1,))],
        compiler_params=pltpu.CompilerParams(vmem_limit_bytes=1024 * 1024),
    )(parts, grad_base)
    if rows < out_rows:
        start = lax.rem(lax.axis_index("tm") * rows, out_rows)
        grad_base = lax.dynamic_slice_in_dim(grad_base, start, rows, 0)
    return grad_noise, grad_base


def solution(mesh):
    n, nz = mesh.shape["tm"], mesh.shape["vocab"]
    return jax.shard_map(
        functools.partial(per_device, n, nz),
        mesh=mesh,
        in_specs=(P("tm", None, "vocab"), P("tm", None, "vocab"), P(None, "vocab"), P()),
        out_specs=(P("tm", None, "vocab"), P("tm", "vocab")),
        check_vma=False,
    )
```

```python
import functools

import jax
import jax.numpy as jnp
from jax import lax
from jax.experimental import pallas as pl
from jax.experimental.pallas import tpu as pltpu
from jax.sharding import PartitionSpec as P

MESH = pl.DeviceIdType.MESH
KC = 16
HB = KC // 2
LANE = 128
FORWARD = (3,3,1,4)
REVERSE = (1,4,4,2)
EARLY = 3
ORDER = [(10, 3), (0, 0), (10, 4), (0, 1), (10, 5), (0, 2), (10, 6), (0, 3), (10, 7), (9, 0), (9, 1), (1, 0), (9, 2), (1, 1), (9, 3), (0, 4), (1, 2), (9, 4), (0, 5), (2, 0), (1, 3), (9, 5), (0, 6), (3, 0), (2, 1), (1, 4), (9, 6), (0, 7), (3, 1), (2, 2), (1, 5), (9, 7), (3, 2), (2, 3), (1, 6), (3, 3), (2, 4), (1, 7), (4, 0), (3, 4), (2, 5), (5, 0), (4, 1), (3, 5), (2, 6), (5, 1), (4, 2), (3, 6), (2, 7), (5, 2), (4, 3), (3, 7), (5, 3), (4, 4), (6, 0), (5, 4), (4, 5), (6, 1), (5, 5), (4, 6), (6, 2), (5, 6), (4, 7), (6, 3), (5, 7), (7, 0), (6, 4), (7, 1), (6, 5), (8, 0), (7, 2), (6, 6), (8, 1), (7, 3), (6, 7), (8, 2), (7, 4), (8, 3), (7, 5), (8, 4), (7, 6), (8, 5), (7, 7), (8, 6), (8, 7)]


def kernel(n, nz, nb, rows, out_rows, dims,
           noise_hbm, counts_hbm, base_hbm, scale_hbm, gn_hbm, gb_hbm,
           noise, counts, base, scale_ref, spread, work, whole, ratio, known, stat, stat_in, tot, tot_out,
           own, mate, src, got, part, share, enter,
           in_sem, out_sem, gb_sem, scale_sem, mate_s, mate_r, hop_s, hop_r, acc_s, acc_r, stat_s, stat_r, tot_s, tot_r):
    T, K, V = dims
    NC = K // KC
    LB = min(256, V)
    VH = V // 2
    per = KC // rows
    me = lax.axis_index("tm")
    z = lax.axis_index("vocab")
    core = lax.rem(me, 2)
    partner = me + 1 - 2 * core
    chip = me // 2

    def bit(j):
        return lax.rem(chip // (2 ** j), 2)

    def across(j):
        return me + (1 - 2 * bit(j)) * (2 ** (j + 1))

    def order(a, j):
        return j if a == 0 else nb - 1 - j

    def upper(p, b):
        return bit(b) == 1 - p

    def above(p, b):
        high = chip // (2 ** (b + 1))
        return high != (0 if p == 0 else 2 ** (nb - 1 - b) - 1)

    def always(x):
        return isinstance(x, bool)

    def sends(p, a, j):
        b = order(a, j)
        if a == 0:
            return True if j < nb - 1 else jnp.logical_not(upper(p, b))
        low = jnp.logical_not(upper(p, b))
        return low if j == 0 else jnp.logical_or(low, above(p, b))

    def receives(p, a, j):
        b = order(a, j)
        if a == 0:
            return True if j < nb - 1 else upper(p, b)
        return upper(p, b) if j == 0 else jnp.logical_or(upper(p, b), above(p, b))

    def guarded(cond, fn):
        if always(cond):
            fn()
        else:
            pl.when(cond)(fn)

    def half(a):
        return pl.ds(a * VH, VH)

    def krows(c):
        return pl.ds(c * KC if isinstance(c, int) else pl.multiple_of(c * KC, KC), KC)

    def load_noise(c):
        return pltpu.make_async_copy(noise_hbm.at[:, krows(c), :], noise.at[c], in_sem.at[c])

    load_counts = pltpu.make_async_copy(counts_hbm, counts, in_sem.at[NC])
    load_base = pltpu.make_async_copy(base_hbm, base, in_sem.at[NC + 1])

    def store_out(c):
        return pltpu.make_async_copy(noise.at[c], gn_hbm.at[c], out_sem.at[0])

    def send(a, b, s, r, device):
        return pltpu.make_async_remote_copy(src_ref=a, dst_ref=b, send_sem=s, recv_sem=r,
                                            device_id=device, device_id_type=MESH)

    def mate_copy(p, c):
        return send(own.at[p, c, 1 - core], mate.at[p, c], mate_s.at[p], mate_r.at[p, c], {"tm": partner})

    def hop_copy(p, a, j, c):
        return send(src.at[p, j, c, :, half(a)], got.at[p, j, c, :, half(a)],
                    hop_s.at[p, a, j], hop_r.at[p, j, c], {"tm": across(order(a, j))})

    def share_copy(p, c):
        return send(share.at[p, c], enter.at[p, c, core], acc_s.at[p], acc_r.at[p, c], {"tm": partner})

    def stat_copy(d, c):
        return send(stat.at[c], stat_in.at[c, d - 1], stat_s.at[d - 1], stat_r.at[c],
                    {"vocab": lax.rem(z + d, nz)})

    def slot():
        return core if per == 1 else 0

    def owner(c, e):
        return c * per + e

    def tot_copy(c, e):
        return send(tot_out.at[c], tot.at[slot()], tot_s.at[c, e], tot_r.at[slot()], {"tm": owner(c, e)})

    def holds(e):
        return chip == 0 if per == 1 else me == (e * rows) // HB

    def each(fn):
        lax.fori_loop(0, NC, lambda i, _: (fn(NC - 1 - i), 0)[1], 0)

    load_scale = pltpu.make_async_copy(scale_hbm, scale_ref, scale_sem.at[0])
    load_scale.start()
    each(lambda c: load_noise(c).start())

    barrier = pltpu.get_barrier_semaphore()
    pl.semaphore_signal(barrier, inc=1, device_id={"tm": partner}, device_id_type=MESH)
    for j in range(nb):
        pl.semaphore_signal(barrier, inc=1, device_id={"tm": across(j)}, device_id_type=MESH)
    for d in range(1, nz):
        pl.semaphore_signal(barrier, inc=1, device_id={"vocab": lax.rem(z + d, nz)}, device_id_type=MESH)
    for h in range(2):
        @pl.when(me != h)
        def _():
            pl.semaphore_signal(barrier, inc=1, device_id={"tm": h}, device_id_type=MESH)

    load_scale.wait()
    wide = jnp.broadcast_to(scale_ref[...], (LANE, LANE)).T
    for c in range(NC):
        spread[c] = wide[c * KC:(c + 1) * KC]

    def lanes(i):
        return pl.ds(pl.multiple_of(i * LB, LB), LB)

    def tiled(x):
        return jnp.concatenate([x] * (LB // LANE), axis=1)

    def two(x):
        return x.reshape(2, HB, x.shape[-1])

    def narrow(sums, e):
        for b in range(LB // LANE):
            sums = sums + e[:, b * LANE:(b + 1) * LANE]
        return sums

    def local(c):
        load_noise(c).wait()
        sp = tiled(spread[c])

        def block(i, _):
            total = jnp.zeros((KC, LB), jnp.float32)
            for t in range(T):
                total = total + noise[c, t, :, lanes(i)].astype(jnp.float32)
            own[0, c, :, :, lanes(i)] = two(sp * total)
            return 0

        lax.fori_loop(0, V // LB, block, 0)

    def expand(c):
        if c == NC - 1:
            load_counts.wait()
        sp = tiled(spread[c])

        def block(i, sums):
            total = jnp.zeros((KC, LB), jnp.float32)
            seen = jnp.zeros((KC, LB), jnp.float32)
            new = []
            for t in range(T):
                total = total + noise[c, t, :, lanes(i)].astype(jnp.float32)
                work[c, t, :, lanes(i)] = jnp.exp(sp * total)
                count = counts[t, krows(c), lanes(i)].astype(jnp.float32)
                seen = seen + count
                new.append(narrow(sums[t], count))
            whole[c, :, lanes(i)] = seen
            return tuple(new)

        sums = lax.fori_loop(0, V // LB, block, tuple(jnp.zeros((KC, LANE), jnp.float32) for _ in range(T)))
        lane = lax.broadcasted_iota(jnp.int32, (KC, LANE), 1)
        packed = jnp.zeros((KC, LANE), jnp.float32)
        for t in range(T):
            packed = jnp.where(lane == T + t, jnp.sum(sums[t], axis=1, keepdims=True), packed)
        known[c] = packed

    def start_hops(p, j, c):
        for a in ((0, 1) if (j + p) % 2 == 0 else (1, 0)):
            guarded(sends(p, a, j), lambda a=a: hop_copy(p, a, j, c).start())

    def first(p, c):
        mate_copy(p, c).wait_recv()
        src[p, 0, c] = own[p, c, core] + mate[p, c]
        part[p, c] = jnp.zeros((HB, V), jnp.float32)
        start_hops(p, 0, c)

    def hop(p, j, c):
        gets = [receives(p, a, j) for a in range(2)]
        if always(gets[0]):
            gets[0] = chip >= 0

        @pl.when(gets[0] & gets[1])
        def _():
            send(got.at[p, j, c], got.at[p, j, c], hop_s.at[p, 0, j], hop_r.at[p, j, c], {"tm": partner}).wait_recv()

        @pl.when(gets[0] != gets[1])
        def _():
            hop_copy(p, 0, j, c).wait_recv()

        for a in range(2):
            up = upper(p, order(a, j))

            def take(a=a, up=up):
                arrived = got[p, j, c, :, half(a)]
                if a == 0:
                    if j < nb - 1:
                        src[p, j + 1, c, :, half(a)] = src[p, j, c, :, half(a)] + arrived
                        arrived = jnp.where(up, arrived, jnp.zeros_like(arrived))
                part[p, c, :, half(a)] = part[p, c, :, half(a)] + arrived

            guarded(receives(p, a, j), take)
        if j < nb - 1:
            low = jnp.logical_not(upper(p, order(1, j + 1)))
            chips = src[p, 0, c, :, half(1)]
            src[p, j + 1, c, :, half(1)] = part[p, c, :, half(1)] + jnp.where(low, chips, jnp.zeros_like(chips))
            start_hops(p, j + 1, c)
            return
        before = part[p, c]
        leads = core == p
        mine, other = own[p, c, core], mate[p, c]
        zero = jnp.zeros_like(before)
        share[p, c] = before + jnp.where(leads, mine, zero)
        enter[p, c, core] = before + jnp.where(leads, zero, other)
        share_copy(p, c).start()
        if p == 1:
            @pl.when(chip == 0)
            def _():
                tot_out[c] = before + src[1, 0, c]
                for e in range(per):
                    @pl.when(holds(e) & (owner(c, e) != me))
                    def _():
                        tot_copy(c, e).start()

                    @pl.when(holds(e) & (owner(c, e) == me))
                    def _():
                        tot[slot()] = tot_out[c]

    def soft(c):
        share_copy(0, c).wait_recv()
        if c == NC - 1:
            load_base.wait()

        def seek(i, top):
            q = base[krows(c), lanes(i)] + enter[0, c, :, :, lanes(i)].reshape(KC, LB)
            base[krows(c), lanes(i)] = q
            for b in range(LB // LANE):
                top = jnp.maximum(top, q[:, b * LANE:(b + 1) * LANE])
            return top

        top = lax.fori_loop(0, V // LB, seek, jnp.full((KC, LANE), -jnp.inf, jnp.float32))
        top = jnp.broadcast_to(jnp.max(top, axis=1, keepdims=True), (KC, LANE))
        tops = tiled(top)

        def block(i, sums):
            w = jnp.exp(base[krows(c), lanes(i)] - tops)
            base[krows(c), lanes(i)] = w
            return tuple(narrow(sums[t], w * work[c, t, :, lanes(i)]) for t in range(T))

        sums = lax.fori_loop(0, V // LB, block, tuple(jnp.zeros((KC, LANE), jnp.float32) for _ in range(T)))
        lane = lax.broadcasted_iota(jnp.int32, (KC, LANE), 1)
        packed = jnp.where(lane < 2 * T, known[c], top)
        for t in range(T):
            packed = jnp.where(lane == t, jnp.sum(sums[t], axis=1, keepdims=True), packed)
        stat[c] = jnp.where(lane[:HB] < LANE // 2, packed[:HB], pltpu.roll(packed[HB:], LANE // 2, 1))
        for d in range(1, nz):
            stat_copy(d, c).start()

    def slopes(c):
        send(stat_in.at[c], stat_in.at[c], stat_s.at[0], stat_r.at[c], {"tm": partner}).wait_recv()
        seen = [stat[c]] + [stat_in[c, d - 1] for d in range(1, nz)]
        tops = [pltpu.roll(x, LANE - 2 * T, 1) for x in seen]
        best, tokens = tops[0], seen[0]
        for d in range(1, nz):
            best = jnp.maximum(best, tops[d])
            tokens = tokens + seen[d]
        factor = [jnp.exp(top - best) for top in tops]
        total = factor[0] * seen[0]
        for d in range(1, nz):
            total = total + factor[d] * seen[d]
        r = factor[0] * pltpu.roll(tokens, LANE - T, 1) / total
        for t in range(T):
            for h in range(2):
                k = h * (LANE // 2) + t
                ratio[c, t, h * HB:(h + 1) * HB] = jnp.broadcast_to(r[:, k:k + 1], (HB, LANE))

        def block(i, _):
            drawn = jnp.zeros((KC, LB), jnp.float32)
            for t in range(T):
                drawn = drawn + tiled(ratio[c, t]) * work[c, t, :, lanes(i)]
            own[1, c, :, :, lanes(i)] = two(whole[c, :, lanes(i)] - base[krows(c), lanes(i)] * drawn)
            return 0

        lax.fori_loop(0, V // LB, block, 0)
        mate_copy(1, c).start()

    def finish(c):
        share_copy(1, c).wait_recv()
        sp = tiled(spread[c])

        def block(i, _):
            w = base[krows(c), lanes(i)]
            run = enter[1, c, :, :, lanes(i)].reshape(KC, LB)
            drawn = jnp.zeros((KC, LB), jnp.float32)
            for t in reversed(range(T)):
                drawn = drawn + tiled(ratio[c, t]) * work[c, t, :, lanes(i)]
                run = run + counts[t, krows(c), lanes(i)].astype(jnp.float32)
                value = sp * (run - w * drawn) - noise[c, t, :, lanes(i)].astype(jnp.float32)
                noise[c, t, :, lanes(i)] = value.astype(jnp.bfloat16)
            return 0

        lax.fori_loop(0, V // LB, block, 0)
        store_out(c).start()

    for k in range(EARLY):
        local(NC - 1 - k)
    load_counts.start()
    load_base.start()
    pl.semaphore_wait(barrier, nb + nz + jnp.where(chip == 0, n - 1, 0))
    for k in range(EARLY):
        mate_copy(0, NC - 1 - k).start()

    def opening(c):
        local(c)
        mate_copy(0, c).start()

    stages = [functools.partial(first, 0), functools.partial(hop, 0, 0), functools.partial(hop, 0, 1), soft, slopes,
              functools.partial(first, 1), functools.partial(hop, 1, 0), functools.partial(hop, 1, 1), finish, expand, opening]
    for st, k in ORDER:
        stages[st](NC - 1 - k)

    begin = me * rows - ((me * rows) // KC) * KC
    if per == 1:
        for h in range(2):
            @pl.when(me != h)
            def _():
                send(tot_out.at[0], tot.at[h], tot_s.at[0, 0], tot_r.at[h], {"tm": h}).wait_recv()
    else:
        @pl.when(me != begin // HB)
        def _():
            send(tot_out.at[0], tot.at[0], tot_s.at[0, 0], tot_r.at[0], {"tm": 0}).wait_recv()
    if per == 1:
        done = [pltpu.make_async_copy(tot.at[h], gb_hbm.at[pl.ds(h * HB, HB), :], gb_sem.at[h]) for h in range(2)]
    else:
        done = [pltpu.make_async_copy(tot.at[0], gb_hbm, gb_sem.at[0])]
    for copy in done:
        copy.start()

    def sent(ref, sem):
        send(ref, ref, sem, hop_r.at[0, 0, 0], {"tm": partner}).wait_send()

    for p in (0, 1):
        sent(mate.at[p], mate_s.at[p])
        sent(share.at[p], acc_s.at[p])
        for a in range(2):
            for j in range(nb):
                guarded(sends(p, a, j), lambda p=p, a=a, j=j: sent(src.at[p, j, :, :, half(a)], hop_s.at[p, a, j]))
    for d in range(1, nz):
        sent(stat, stat_s.at[d - 1])

    def drain(c):
        for e in range(per):
            @pl.when((chip == 0) & holds(e) & (owner(c, e) != me))
            def _():
                tot_copy(c, e).wait_send()

    each(drain)
    pltpu.make_async_copy(noise, gn_hbm, out_sem.at[0]).wait()
    for copy in done:
        copy.wait()


def place(parts, base, gn_hbm, gb_hbm, sem):
    NC = parts.shape[0]
    copies = [pltpu.make_async_copy(parts.at[c], gn_hbm.at[:, pl.ds(c * KC, KC), :], sem.at[c]) for c in range(NC)]
    copies.append(pltpu.make_async_copy(base, gb_hbm, sem.at[NC]))
    for copy in copies:
        copy.start()
    for copy in copies:
        copy.wait()


def per_device(n, nz, drift_noise, counts, base_logits, drift_scale):
    T, K, V = drift_noise.shape
    nb = n.bit_length() - 2
    rows = K // n
    out_rows = KC if rows >= KC else HB
    NC = K // KC
    f32, bf16 = jnp.float32, jnp.bfloat16
    dma = pltpu.SemaphoreType.DMA
    any_space = pl.BlockSpec(memory_space=pl.ANY)
    peers = max(nz - 1, 1)
    parts, grad_base = pl.pallas_call(
        functools.partial(kernel, n, nz, nb, rows, out_rows, (T, K, V)),
        out_shape=(jax.ShapeDtypeStruct((NC, T, KC, V), bf16), jax.ShapeDtypeStruct((out_rows, V), f32)),
        in_specs=[any_space] * 4,
        out_specs=(any_space, any_space),
        scratch_shapes=[
            pltpu.VMEM((NC, T, KC, V), bf16),
            pltpu.VMEM((T, K, V), bf16),
            pltpu.VMEM((K, V), f32),
            pltpu.VMEM((1, K), f32),
            pltpu.VMEM((NC, KC, LANE), f32),
            pltpu.VMEM((NC, T, KC, V), f32),
            pltpu.VMEM((NC, KC, V), f32),
            pltpu.VMEM((NC, T, KC, LANE), f32),
            pltpu.VMEM((NC, KC, LANE), f32),
            pltpu.VMEM((NC, HB, LANE), f32),
            pltpu.VMEM((NC, peers, HB, LANE), f32),
            pltpu.VMEM((2, HB, V), f32),
            pltpu.VMEM((NC, HB, V), f32),
            pltpu.VMEM((2, NC, 2, HB, V), f32),
            pltpu.VMEM((2, NC, HB, V), f32),
            pltpu.VMEM((2, nb, NC, HB, V), f32),
            pltpu.VMEM((2, nb, NC, HB, V), f32),
            pltpu.VMEM((2, NC, HB, V), f32),
            pltpu.VMEM((2, NC, HB, V), f32),
            pltpu.VMEM((2, NC, 2, HB, V), f32),
            dma((NC + 2,)), dma((1,)), dma((2,)), dma((1,)),
            dma((2,)), dma((2, NC)),
            dma((2, 2, nb)), dma((2, nb, NC)),
            dma((2,)), dma((2, NC)),
            dma((peers,)), dma((NC,)),
            dma((NC, KC // rows)), dma((2,)),
        ],
        compiler_params=pltpu.CompilerParams(
            collective_id=0, has_side_effects=True, vmem_limit_bytes=46 * 1024 * 1024),
    )(*[pltpu.with_memory_space_constraint(x, pltpu.HBM) for x in (drift_noise, counts, base_logits, drift_scale.reshape(1, K))])
    grad_noise, grad_base = pl.pallas_call(
        place,
        out_shape=(jax.ShapeDtypeStruct((T, K, V), bf16), jax.ShapeDtypeStruct((out_rows, V), f32)),
        in_specs=[any_space] * 2,
        out_specs=(any_space, any_space),
        scratch_shapes=[dma((NC + 1,))],
        compiler_params=pltpu.CompilerParams(vmem_limit_bytes=1024 * 1024),
    )(parts, grad_base)
    if rows < out_rows:
        start = lax.rem(lax.axis_index("tm") * rows, out_rows)
        grad_base = lax.dynamic_slice_in_dim(grad_base, start, rows, 0)
    return grad_noise, grad_base


def solution(mesh):
    n, nz = mesh.shape["tm"], mesh.shape["vocab"]
    return jax.shard_map(
        functools.partial(per_device, n, nz),
        mesh=mesh,
        in_specs=(P("tm", None, "vocab"), P("tm", None, "vocab"), P(None, "vocab"), P()),
        out_specs=(P("tm", None, "vocab"), P("tm", "vocab")),
        check_vma=False,
    )
```

```python
import functools

import jax
import jax.numpy as jnp
from jax import lax
from jax.experimental import pallas as pl
from jax.experimental.pallas import tpu as pltpu
from jax.sharding import PartitionSpec as P

MESH = pl.DeviceIdType.MESH
KC = 16
HB = KC // 2
LANE = 128
FORWARD = (3,3,1,4)
REVERSE = (1,4,4,2)
EARLY = 3
ORDER = [(10, 3), (0, 0), (10, 4), (0, 1), (10, 5), (0, 2), (10, 6), (0, 3), (10, 7), (9, 0), (9, 1), (9, 2), (0, 4), (9, 3), (1, 0), (0, 5), (9, 4), (1, 1), (0, 6), (9, 5), (1, 2), (0, 7), (9, 6), (9, 7), (1, 3), (2, 0), (1, 4), (2, 1), (1, 5), (3, 0), (2, 2), (1, 6), (3, 1), (2, 3), (1, 7), (3, 2), (2, 4), (3, 3), (2, 5), (3, 4), (2, 6), (4, 0), (3, 5), (2, 7), (4, 1), (3, 6), (5, 0), (4, 2), (3, 7), (5, 1), (4, 3), (5, 2), (4, 4), (5, 3), (4, 5), (5, 4), (4, 6), (6, 0), (5, 5), (4, 7), (6, 1), (5, 6), (6, 2), (5, 7), (6, 3), (6, 4), (7, 0), (6, 5), (7, 1), (6, 6), (8, 0), (7, 2), (6, 7), (8, 1), (7, 3), (8, 2), (7, 4), (8, 3), (7, 5), (8, 4), (7, 6), (8, 5), (7, 7), (8, 6), (8, 7)]


def kernel(n, nz, nb, rows, out_rows, dims,
           noise_hbm, counts_hbm, base_hbm, scale_hbm, gn_hbm, gb_hbm,
           noise, counts, base, scale_ref, spread, work, whole, ratio, known, stat, stat_in, tot, tot_out,
           own, mate, src, got, part, share, enter,
           in_sem, out_sem, gb_sem, scale_sem, mate_s, mate_r, hop_s, hop_r, acc_s, acc_r, stat_s, stat_r, tot_s, tot_r):
    T, K, V = dims
    NC = K // KC
    LB = min(512, V)
    VH = V // 2
    per = KC // rows
    me = lax.axis_index("tm")
    z = lax.axis_index("vocab")
    core = lax.rem(me, 2)
    partner = me + 1 - 2 * core
    chip = me // 2

    def bit(j):
        return lax.rem(chip // (2 ** j), 2)

    def across(j):
        return me + (1 - 2 * bit(j)) * (2 ** (j + 1))

    def order(a, j):
        return j if a == 0 else nb - 1 - j

    def upper(p, b):
        return bit(b) == 1 - p

    def above(p, b):
        high = chip // (2 ** (b + 1))
        return high != (0 if p == 0 else 2 ** (nb - 1 - b) - 1)

    def always(x):
        return isinstance(x, bool)

    def sends(p, a, j):
        b = order(a, j)
        if a == 0:
            return True if j < nb - 1 else jnp.logical_not(upper(p, b))
        low = jnp.logical_not(upper(p, b))
        return low if j == 0 else jnp.logical_or(low, above(p, b))

    def receives(p, a, j):
        b = order(a, j)
        if a == 0:
            return True if j < nb - 1 else upper(p, b)
        return upper(p, b) if j == 0 else jnp.logical_or(upper(p, b), above(p, b))

    def guarded(cond, fn):
        if always(cond):
            fn()
        else:
            pl.when(cond)(fn)

    def half(a):
        return pl.ds(a * VH, VH)

    def krows(c):
        return pl.ds(c * KC if isinstance(c, int) else pl.multiple_of(c * KC, KC), KC)

    def load_noise(c):
        return pltpu.make_async_copy(noise_hbm.at[:, krows(c), :], noise.at[c], in_sem.at[c])

    load_counts = pltpu.make_async_copy(counts_hbm, counts, in_sem.at[NC])
    load_base = pltpu.make_async_copy(base_hbm, base, in_sem.at[NC + 1])

    def store_out(c):
        return pltpu.make_async_copy(noise.at[c], gn_hbm.at[c], out_sem.at[0])

    def send(a, b, s, r, device):
        return pltpu.make_async_remote_copy(src_ref=a, dst_ref=b, send_sem=s, recv_sem=r,
                                            device_id=device, device_id_type=MESH)

    def mate_copy(p, c):
        return send(own.at[p, c, 1 - core], mate.at[p, c], mate_s.at[p], mate_r.at[c], {"tm": partner})

    def hop_copy(p, a, j, c):
        return send(src.at[p, j, c, :, half(a)], got.at[p, j, c, :, half(a)],
                    hop_s.at[p, a, j], hop_r.at[p, j, c], {"tm": across(order(a, j))})

    def share_copy(p, c):
        return send(share.at[p, c], enter.at[p, c, core], acc_s.at[p], acc_r.at[c], {"tm": partner})

    def stat_copy(d, c):
        return send(stat.at[c], stat_in.at[c, d - 1], stat_s.at[d - 1], stat_r.at[c],
                    {"vocab": lax.rem(z + d, nz)})

    def slot():
        return core if per == 1 else 0

    def owner(c, e):
        return c * per + e

    def tot_copy(c, e):
        return send(tot_out.at[c], tot.at[slot()], tot_s.at[c, e], tot_r.at[slot()], {"tm": owner(c, e)})

    def holds(e):
        return chip == 0 if per == 1 else me == (e * rows) // HB

    def each(fn):
        lax.fori_loop(0, NC, lambda i, _: (fn(NC - 1 - i), 0)[1], 0)

    barrier = pltpu.get_barrier_semaphore()
    for d in range(nz - 1, 0, -1):
        pl.semaphore_signal(barrier, inc=1, device_id={"vocab": lax.rem(z + d, nz)}, device_id_type=MESH)
    for h in range(2):
        @pl.when(me != h)
        def _():
            pl.semaphore_signal(barrier, inc=1, device_id={"tm": h}, device_id_type=MESH)
    pl.semaphore_signal(barrier, inc=1, device_id={"tm": partner}, device_id_type=MESH)
    for j in range(nb):
        pl.semaphore_signal(barrier, inc=1, device_id={"tm": across(j)}, device_id_type=MESH)

    load_scale = pltpu.make_async_copy(scale_hbm, scale_ref, scale_sem.at[0])
    load_scale.start()
    each(lambda c: load_noise(c).start())

    load_scale.wait()
    wide = jnp.broadcast_to(scale_ref[...], (LANE, LANE)).T
    for c in range(NC):
        spread[c] = wide[c * KC:(c + 1) * KC]

    def lanes(i):
        return pl.ds(pl.multiple_of(i * LB, LB), LB)

    def tiled(x):
        return jnp.concatenate([x] * (LB // LANE), axis=1)

    def two(x):
        return x.reshape(2, HB, x.shape[-1])

    def narrow(sums, e):
        for b in range(LB // LANE):
            sums = sums + e[:, b * LANE:(b + 1) * LANE]
        return sums

    def local(c):
        load_noise(c).wait()
        sp = tiled(spread[c])

        def block(i, _):
            total = jnp.zeros((KC, LB), jnp.float32)
            for t in range(T):
                total = total + noise[c, t, :, lanes(i)].astype(jnp.float32)
            own[0, c, :, :, lanes(i)] = two(sp * total)
            return 0

        lax.fori_loop(0, V // LB, block, 0)

    def expand(c):
        if c == NC - 1:
            load_counts.wait()
        sp = tiled(spread[c])

        def block(i, sums):
            total = jnp.zeros((KC, LB), jnp.float32)
            seen = jnp.zeros((KC, LB), jnp.float32)
            new = []
            for t in range(T):
                total = total + noise[c, t, :, lanes(i)].astype(jnp.float32)
                work[c, t, :, lanes(i)] = jnp.exp(sp * total)
                count = counts[t, krows(c), lanes(i)].astype(jnp.float32)
                seen = seen + count
                new.append(narrow(sums[t], count))
            whole[c, :, lanes(i)] = seen
            return tuple(new)

        sums = lax.fori_loop(0, V // LB, block, tuple(jnp.zeros((KC, LANE), jnp.float32) for _ in range(T)))
        lane = lax.broadcasted_iota(jnp.int32, (KC, LANE), 1)
        packed = jnp.zeros((KC, LANE), jnp.float32)
        for t in range(T):
            packed = jnp.where(lane == T + t, jnp.sum(sums[t], axis=1, keepdims=True), packed)
        known[c] = packed

    def start_hops(p, j, c):
        for a in ((0, 1) if (j + p) % 2 == 0 else (1, 0)):
            guarded(sends(p, a, j), lambda a=a: hop_copy(p, a, j, c).start())

    def first(p, c):
        mate_copy(p, c).wait_recv()
        src[p, 0, c] = own[p, c, core] + mate[p, c]
        part[p, c] = jnp.zeros((HB, V), jnp.float32)
        start_hops(p, 0, c)

    def hop(p, j, c):
        gets = [receives(p, a, j) for a in range(2)]
        if always(gets[0]):
            gets[0] = chip >= 0

        @pl.when(gets[0] & gets[1])
        def _():
            send(got.at[p, j, c], got.at[p, j, c], hop_s.at[p, 0, j], hop_r.at[p, j, c], {"tm": partner}).wait_recv()

        @pl.when(gets[0] != gets[1])
        def _():
            hop_copy(p, 0, j, c).wait_recv()

        for a in range(2):
            up = upper(p, order(a, j))

            def take(a=a, up=up):
                arrived = got[p, j, c, :, half(a)]
                if a == 0:
                    if j < nb - 1:
                        src[p, j + 1, c, :, half(a)] = src[p, j, c, :, half(a)] + arrived
                        arrived = jnp.where(up, arrived, jnp.zeros_like(arrived))
                part[p, c, :, half(a)] = part[p, c, :, half(a)] + arrived

            guarded(receives(p, a, j), take)
        if j < nb - 1:
            low = jnp.logical_not(upper(p, order(1, j + 1)))
            chips = src[p, 0, c, :, half(1)]
            src[p, j + 1, c, :, half(1)] = part[p, c, :, half(1)] + jnp.where(low, chips, jnp.zeros_like(chips))
            start_hops(p, j + 1, c)
            return
        before = part[p, c]
        leads = core == p
        mine, other = own[p, c, core], mate[p, c]
        zero = jnp.zeros_like(before)
        share[p, c] = before + jnp.where(leads, mine, zero)
        enter[p, c, core] = before + jnp.where(leads, zero, other)
        share_copy(p, c).start()
        if p == 1:
            @pl.when(chip == 0)
            def _():
                tot_out[c] = before + src[1, 0, c]
                for e in range(per):
                    @pl.when(holds(e) & (owner(c, e) != me))
                    def _():
                        tot_copy(c, e).start()

                    @pl.when(holds(e) & (owner(c, e) == me))
                    def _():
                        tot[slot()] = tot_out[c]

    def soft(c):
        share_copy(0, c).wait_recv()
        if c == NC - 1:
            load_base.wait()

        def seek(i, top):
            q = base[krows(c), lanes(i)] + enter[0, c, :, :, lanes(i)].reshape(KC, LB)
            base[krows(c), lanes(i)] = q
            for b in range(LB // LANE):
                top = jnp.maximum(top, q[:, b * LANE:(b + 1) * LANE])
            return top

        top = lax.fori_loop(0, V // LB, seek, jnp.full((KC, LANE), -jnp.inf, jnp.float32))
        top = jnp.broadcast_to(jnp.max(top, axis=1, keepdims=True), (KC, LANE))
        tops = tiled(top)

        def block(i, sums):
            w = jnp.exp(base[krows(c), lanes(i)] - tops)
            base[krows(c), lanes(i)] = w
            return tuple(narrow(sums[t], w * work[c, t, :, lanes(i)]) for t in range(T))

        sums = lax.fori_loop(0, V // LB, block, tuple(jnp.zeros((KC, LANE), jnp.float32) for _ in range(T)))
        lane = lax.broadcasted_iota(jnp.int32, (KC, LANE), 1)
        packed = jnp.where(lane < 2 * T, known[c], top)
        for t in range(T):
            packed = jnp.where(lane == t, jnp.sum(sums[t], axis=1, keepdims=True), packed)
        stat[c] = jnp.where(lane[:HB] < LANE // 2, packed[:HB], pltpu.roll(packed[HB:], LANE // 2, 1))
        for d in range(1, nz):
            stat_copy(d, c).start()

    def slopes(c):
        send(stat_in.at[c], stat_in.at[c], stat_s.at[0], stat_r.at[c], {"tm": partner}).wait_recv()
        seen = [stat[c]] + [stat_in[c, d - 1] for d in range(1, nz)]
        tops = [pltpu.roll(x, LANE - 2 * T, 1) for x in seen]
        best, tokens = tops[0], seen[0]
        for d in range(1, nz):
            best = jnp.maximum(best, tops[d])
            tokens = tokens + seen[d]
        factor = [jnp.exp(top - best) for top in tops]
        total = factor[0] * seen[0]
        for d in range(1, nz):
            total = total + factor[d] * seen[d]
        r = factor[0] * pltpu.roll(tokens, LANE - T, 1) / total
        for t in range(T):
            for h in range(2):
                k = h * (LANE // 2) + t
                ratio[c, t, h * HB:(h + 1) * HB] = jnp.broadcast_to(r[:, k:k + 1], (HB, LANE))

        def block(i, _):
            drawn = jnp.zeros((KC, LB), jnp.float32)
            for t in range(T):
                drawn = drawn + tiled(ratio[c, t]) * work[c, t, :, lanes(i)]
            own[1, c, :, :, lanes(i)] = two(whole[c, :, lanes(i)] - base[krows(c), lanes(i)] * drawn)
            return 0

        lax.fori_loop(0, V // LB, block, 0)
        mate_copy(1, c).start()

    def finish(c):
        share_copy(1, c).wait_recv()
        sp = tiled(spread[c])

        def block(i, _):
            w = base[krows(c), lanes(i)]
            run = enter[1, c, :, :, lanes(i)].reshape(KC, LB)
            drawn = jnp.zeros((KC, LB), jnp.float32)
            for t in reversed(range(T)):
                drawn = drawn + tiled(ratio[c, t]) * work[c, t, :, lanes(i)]
                run = run + counts[t, krows(c), lanes(i)].astype(jnp.float32)
                value = sp * (run - w * drawn) - noise[c, t, :, lanes(i)].astype(jnp.float32)
                noise[c, t, :, lanes(i)] = value.astype(jnp.bfloat16)
            return 0

        lax.fori_loop(0, V // LB, block, 0)
        store_out(c).start()

    for k in range(EARLY):
        local(NC - 1 - k)
    load_counts.start()
    load_base.start()
    pl.semaphore_wait(barrier, nb + nz + jnp.where(chip == 0, n - 1, 0))
    for k in range(EARLY):
        mate_copy(0, NC - 1 - k).start()

    def opening(c):
        local(c)
        mate_copy(0, c).start()

    stages = [functools.partial(first, 0), functools.partial(hop, 0, 0), functools.partial(hop, 0, 1), soft, slopes,
              functools.partial(first, 1), functools.partial(hop, 1, 0), functools.partial(hop, 1, 1), finish, expand, opening]
    for st, k in ORDER:
        stages[st](NC - 1 - k)

    begin = me * rows - ((me * rows) // KC) * KC
    if per == 1:
        for h in range(2):
            @pl.when(me != h)
            def _():
                send(tot_out.at[0], tot.at[h], tot_s.at[0, 0], tot_r.at[h], {"tm": h}).wait_recv()
    else:
        @pl.when(me != begin // HB)
        def _():
            send(tot_out.at[0], tot.at[0], tot_s.at[0, 0], tot_r.at[0], {"tm": 0}).wait_recv()
    if per == 1:
        done = [pltpu.make_async_copy(tot.at[h], gb_hbm.at[pl.ds(h * HB, HB), :], gb_sem.at[h]) for h in range(2)]
    else:
        done = [pltpu.make_async_copy(tot.at[0], gb_hbm, gb_sem.at[0])]
    for copy in done:
        copy.start()

    def sent(ref, sem):
        send(ref, ref, sem, hop_r.at[0, 0, 0], {"tm": partner}).wait_send()

    for p in (0, 1):
        sent(mate.at[p], mate_s.at[p])
        sent(share.at[p], acc_s.at[p])
        for a in range(2):
            for j in range(nb):
                guarded(sends(p, a, j), lambda p=p, a=a, j=j: sent(src.at[p, j, :, :, half(a)], hop_s.at[p, a, j]))
    for d in range(1, nz):
        sent(stat, stat_s.at[d - 1])

    def drain(c):
        for e in range(per):
            @pl.when((chip == 0) & holds(e) & (owner(c, e) != me))
            def _():
                tot_copy(c, e).wait_send()

    each(drain)
    pltpu.make_async_copy(noise, gn_hbm, out_sem.at[0]).wait()
    for copy in done:
        copy.wait()


def place(parts, base, gn_hbm, gb_hbm, sem):
    NC = parts.shape[0]
    copies = [pltpu.make_async_copy(parts.at[c], gn_hbm.at[:, pl.ds(c * KC, KC), :], sem.at[c]) for c in range(NC)]
    copies.append(pltpu.make_async_copy(base, gb_hbm, sem.at[NC]))
    for copy in copies:
        copy.start()
    for copy in copies:
        copy.wait()


def per_device(n, nz, drift_noise, counts, base_logits, drift_scale):
    T, K, V = drift_noise.shape
    nb = n.bit_length() - 2
    rows = K // n
    out_rows = KC if rows >= KC else HB
    NC = K // KC
    f32, bf16 = jnp.float32, jnp.bfloat16
    dma = pltpu.SemaphoreType.DMA
    any_space = pl.BlockSpec(memory_space=pl.ANY)
    peers = max(nz - 1, 1)
    parts, grad_base = pl.pallas_call(
        functools.partial(kernel, n, nz, nb, rows, out_rows, (T, K, V)),
        out_shape=(jax.ShapeDtypeStruct((NC, T, KC, V), bf16), jax.ShapeDtypeStruct((out_rows, V), f32)),
        in_specs=[any_space] * 4,
        out_specs=(any_space, any_space),
        scratch_shapes=[
            pltpu.VMEM((NC, T, KC, V), bf16),
            pltpu.VMEM((T, K, V), bf16),
            pltpu.VMEM((K, V), f32),
            pltpu.VMEM((1, K), f32),
            pltpu.VMEM((NC, KC, LANE), f32),
            pltpu.VMEM((NC, T, KC, V), f32),
            pltpu.VMEM((NC, KC, V), f32),
            pltpu.VMEM((NC, T, KC, LANE), f32),
            pltpu.VMEM((NC, KC, LANE), f32),
            pltpu.VMEM((NC, HB, LANE), f32),
            pltpu.VMEM((NC, peers, HB, LANE), f32),
            pltpu.VMEM((2, HB, V), f32),
            pltpu.VMEM((NC, HB, V), f32),
            pltpu.VMEM((2, NC, 2, HB, V), f32),
            pltpu.VMEM((2, NC, HB, V), f32),
            pltpu.VMEM((2, nb, NC, HB, V), f32),
            pltpu.VMEM((2, nb, NC, HB, V), f32),
            pltpu.VMEM((2, NC, HB, V), f32),
            pltpu.VMEM((2, NC, HB, V), f32),
            pltpu.VMEM((2, NC, 2, HB, V), f32),
            dma((NC + 2,)), dma((1,)), dma((2,)), dma((1,)),
            dma((2,)), dma((NC,)),
            dma((2, 2, nb)), dma((2, nb, NC)),
            dma((2,)), dma((NC,)),
            dma((peers,)), dma((NC,)),
            dma((NC, KC // rows)), dma((2,)),
        ],
        compiler_params=pltpu.CompilerParams(
            collective_id=0, has_side_effects=True, vmem_limit_bytes=46 * 1024 * 1024),
    )(*[pltpu.with_memory_space_constraint(x, pltpu.HBM) for x in (drift_noise, counts, base_logits, drift_scale.reshape(1, K))])
    grad_noise, grad_base = pl.pallas_call(
        place,
        out_shape=(jax.ShapeDtypeStruct((T, K, V), bf16), jax.ShapeDtypeStruct((out_rows, V), f32)),
        in_specs=[any_space] * 2,
        out_specs=(any_space, any_space),
        scratch_shapes=[dma((NC + 1,))],
        compiler_params=pltpu.CompilerParams(vmem_limit_bytes=1024 * 1024),
    )(parts, grad_base)
    if rows < out_rows:
        start = lax.rem(lax.axis_index("tm") * rows, out_rows)
        grad_base = lax.dynamic_slice_in_dim(grad_base, start, rows, 0)
    return grad_noise, grad_base


def solution(mesh):
    n, nz = mesh.shape["tm"], mesh.shape["vocab"]
    return jax.shard_map(
        functools.partial(per_device, n, nz),
        mesh=mesh,
        in_specs=(P("tm", None, "vocab"), P("tm", None, "vocab"), P(None, "vocab"), P()),
        out_specs=(P("tm", None, "vocab"), P("tm", "vocab")),
        check_vma=False,
    )
```

```python
import functools

import jax
import jax.numpy as jnp
from jax import lax
from jax.experimental import pallas as pl
from jax.experimental.pallas import tpu as pltpu
from jax.sharding import PartitionSpec as P

MESH = pl.DeviceIdType.MESH
KC = 16
HB = KC // 2
LANE = 128
EARLY = 3
ORDER = [(10, 3), (0, 0), (10, 4), (0, 1), (10, 5), (0, 2), (10, 6), (0, 3), (10, 7), (9, 0), (9, 1), (9, 2), (0, 4), (9, 3), (1, 0), (0, 5), (9, 4), (1, 1), (0, 6), (9, 5), (1, 2), (0, 7), (9, 6), (9, 7), (1, 3), (1, 4), (2, 0), (1, 5), (2, 1), (3, 0), (1, 6), (2, 2), (3, 1), (1, 7), (2, 3), (3, 2), (2, 4), (3, 3), (2, 5), (3, 4), (2, 6), (4, 0), (3, 5), (2, 7), (4, 1), (3, 6), (5, 0), (4, 2), (3, 7), (5, 1), (4, 3), (5, 2), (4, 4), (5, 3), (4, 5), (5, 4), (4, 6), (5, 5), (4, 7), (6, 0), (5, 6), (6, 1), (5, 7), (6, 2), (6, 3), (6, 4), (6, 5), (7, 0), (6, 6), (7, 1), (6, 7), (7, 2), (8, 0), (7, 3), (8, 1), (7, 4), (8, 2), (7, 5), (8, 3), (7, 6), (8, 4), (7, 7), (8, 5), (8, 6), (8, 7)]


def kernel(n, nz, nb, rows, out_rows, dims,
           noise_hbm, counts_hbm, base_hbm, scale_hbm, gn_hbm, gb_hbm,
           noise, counts, base, scale_ref, spread, work, whole, ratio, known, stat, stat_in, tot, tot_out,
           own, mate, src, got, part, share, enter,
           in_sem, out_sem, gb_sem, scale_sem, mate_s, mate_r, hop_s, hop_r, acc_s, acc_r, stat_s, stat_r, tot_s, tot_r):
    T, K, V = dims
    NC = K // KC
    LB = min(512, V)
    VH = V // 2
    per = KC // rows
    me = lax.axis_index("tm")
    z = lax.axis_index("vocab")
    core = lax.rem(me, 2)
    partner = me + 1 - 2 * core
    chip = me // 2

    def bit(j):
        return lax.rem(chip // (2 ** j), 2)

    def across(j):
        return me + (1 - 2 * bit(j)) * (2 ** (j + 1))

    def order(a, j):
        return j if a == 0 else nb - 1 - j

    def upper(p, b):
        return bit(b) == 1 - p

    def above(p, b):
        high = chip // (2 ** (b + 1))
        return high != (0 if p == 0 else 2 ** (nb - 1 - b) - 1)

    def always(x):
        return isinstance(x, bool)

    def sends(p, a, j):
        b = order(a, j)
        if a == 0:
            return True if j < nb - 1 else jnp.logical_not(upper(p, b))
        low = jnp.logical_not(upper(p, b))
        return low if j == 0 else jnp.logical_or(low, above(p, b))

    def receives(p, a, j):
        b = order(a, j)
        if a == 0:
            return True if j < nb - 1 else upper(p, b)
        return upper(p, b) if j == 0 else jnp.logical_or(upper(p, b), above(p, b))

    def guarded(cond, fn):
        if always(cond):
            fn()
        else:
            pl.when(cond)(fn)

    def half(a):
        return pl.ds(a * VH, VH)

    def krows(c):
        return pl.ds(c * KC if isinstance(c, int) else pl.multiple_of(c * KC, KC), KC)

    def load_noise(c):
        return pltpu.make_async_copy(noise_hbm.at[:, krows(c), :], noise.at[c], in_sem.at[c])

    load_counts = pltpu.make_async_copy(counts_hbm, counts, in_sem.at[NC])
    load_base = pltpu.make_async_copy(base_hbm, base, in_sem.at[NC + 1])

    def store_out(c):
        return pltpu.make_async_copy(noise.at[c], gn_hbm.at[c], out_sem.at[0])

    def send(a, b, s, r, device):
        return pltpu.make_async_remote_copy(src_ref=a, dst_ref=b, send_sem=s, recv_sem=r,
                                            device_id=device, device_id_type=MESH)

    def mate_copy(p, c):
        return send(own.at[p, c, 1 - core], mate.at[p, c], mate_s.at[p], mate_r.at[c], {"tm": partner})

    def hop_copy(p, a, j, c):
        return send(src.at[p, j, c, :, half(a)], got.at[p, j, c, :, half(a)],
                    hop_s.at[p, a, j], hop_r.at[p, j, c], {"tm": across(order(a, j))})

    def share_copy(p, c):
        return send(share.at[p, c], enter.at[p, c, core], acc_s.at[p], acc_r.at[c], {"tm": partner})

    def stat_copy(d, c):
        return send(stat.at[c], stat_in.at[c, d - 1], stat_s.at[d - 1], stat_r.at[c],
                    {"vocab": lax.rem(z + d, nz)})

    def slot():
        return core if per == 1 else 0

    def owner(c, e):
        return c * per + e

    def tot_copy(c, e):
        return send(tot_out.at[c], tot.at[slot()], tot_s.at[c, e], tot_r.at[slot()], {"tm": owner(c, e)})

    def holds(e):
        return chip == 0 if per == 1 else me == (e * rows) // HB

    def each(fn):
        lax.fori_loop(0, NC, lambda i, _: (fn(NC - 1 - i), 0)[1], 0)

    barrier = pltpu.get_barrier_semaphore()
    for d in range(nz - 1, 0, -1):
        pl.semaphore_signal(barrier, inc=1, device_id={"vocab": lax.rem(z + d, nz)}, device_id_type=MESH)
    for h in range(2):
        @pl.when(me != h)
        def _():
            pl.semaphore_signal(barrier, inc=1, device_id={"tm": h}, device_id_type=MESH)
    pl.semaphore_signal(barrier, inc=1, device_id={"tm": partner}, device_id_type=MESH)
    for j in range(nb):
        pl.semaphore_signal(barrier, inc=1, device_id={"tm": across(j)}, device_id_type=MESH)

    load_scale = pltpu.make_async_copy(scale_hbm, scale_ref, scale_sem.at[0])
    load_scale.start()
    each(lambda c: load_noise(c).start())

    load_scale.wait()
    wide = jnp.broadcast_to(scale_ref[...], (LANE, LANE)).T
    for c in range(NC):
        spread[c] = wide[c * KC:(c + 1) * KC]

    def lanes(i):
        return pl.ds(pl.multiple_of(i * LB, LB), LB)

    def tiled(x):
        return jnp.concatenate([x] * (LB // LANE), axis=1)

    def two(x):
        return x.reshape(2, HB, x.shape[-1])

    def narrow(sums, e):
        for b in range(LB // LANE):
            sums = sums + e[:, b * LANE:(b + 1) * LANE]
        return sums

    def local(c):
        load_noise(c).wait()
        sp = tiled(spread[c])

        def block(i, _):
            total = jnp.zeros((KC, LB), jnp.float32)
            for t in range(T):
                total = total + noise[c, t, :, lanes(i)].astype(jnp.float32)
            own[0, c, :, :, lanes(i)] = two(sp * total)
            return 0

        lax.fori_loop(0, V // LB, block, 0)

    def expand(c):
        if c == NC - 1:
            load_counts.wait()
        sp = tiled(spread[c])

        def block(i, sums):
            total = jnp.zeros((KC, LB), jnp.float32)
            seen = jnp.zeros((KC, LB), jnp.float32)
            new = []
            for t in range(T):
                total = total + noise[c, t, :, lanes(i)].astype(jnp.float32)
                work[c, t, :, lanes(i)] = jnp.exp(sp * total)
                count = counts[t, krows(c), lanes(i)].astype(jnp.float32)
                seen = seen + count
                new.append(narrow(sums[t], count))
            whole[c, :, lanes(i)] = seen
            return tuple(new)

        sums = lax.fori_loop(0, V // LB, block, tuple(jnp.zeros((KC, LANE), jnp.float32) for _ in range(T)))
        lane = lax.broadcasted_iota(jnp.int32, (KC, LANE), 1)
        packed = jnp.zeros((KC, LANE), jnp.float32)
        for t in range(T):
            packed = jnp.where(lane == T + t, jnp.sum(sums[t], axis=1, keepdims=True), packed)
        known[c] = packed

    def start_hops(p, j, c):
        for a in ((0, 1) if (j + p) % 2 == 0 else (1, 0)):
            guarded(sends(p, a, j), lambda a=a: hop_copy(p, a, j, c).start())

    def first(p, c):
        mate_copy(p, c).wait_recv()
        src[p, 0, c] = own[p, c, core] + mate[p, c]
        part[p, c] = jnp.zeros((HB, V), jnp.float32)
        start_hops(p, 0, c)

    def hop(p, j, c):
        gets = [receives(p, a, j) for a in range(2)]
        if always(gets[0]):
            gets[0] = chip >= 0

        @pl.when(gets[0] & gets[1])
        def _():
            send(got.at[p, j, c], got.at[p, j, c], hop_s.at[p, 0, j], hop_r.at[p, j, c], {"tm": partner}).wait_recv()

        @pl.when(gets[0] != gets[1])
        def _():
            hop_copy(p, 0, j, c).wait_recv()

        for a in range(2):
            up = upper(p, order(a, j))

            def take(a=a, up=up):
                arrived = got[p, j, c, :, half(a)]
                if a == 0:
                    if j < nb - 1:
                        src[p, j + 1, c, :, half(a)] = src[p, j, c, :, half(a)] + arrived
                        arrived = jnp.where(up, arrived, jnp.zeros_like(arrived))
                part[p, c, :, half(a)] = part[p, c, :, half(a)] + arrived

            guarded(receives(p, a, j), take)
        if j < nb - 1:
            low = jnp.logical_not(upper(p, order(1, j + 1)))
            chips = src[p, 0, c, :, half(1)]
            src[p, j + 1, c, :, half(1)] = part[p, c, :, half(1)] + jnp.where(low, chips, jnp.zeros_like(chips))
            start_hops(p, j + 1, c)
            return
        before = part[p, c]
        leads = core == p
        mine, other = own[p, c, core], mate[p, c]
        zero = jnp.zeros_like(before)
        share[p, c] = before + jnp.where(leads, mine, zero)
        enter[p, c, core] = before + jnp.where(leads, zero, other)
        share_copy(p, c).start()
        if p == 1:
            @pl.when(chip == 0)
            def _():
                tot_out[c] = before + src[1, 0, c]
                for e in range(per):
                    @pl.when(holds(e) & (owner(c, e) != me))
                    def _():
                        tot_copy(c, e).start()

                    @pl.when(holds(e) & (owner(c, e) == me))
                    def _():
                        tot[slot()] = tot_out[c]

    def soft(c):
        share_copy(0, c).wait_recv()
        if c == NC - 1:
            load_base.wait()

        def seek(i, top):
            q = base[krows(c), lanes(i)] + enter[0, c, :, :, lanes(i)].reshape(KC, LB)
            base[krows(c), lanes(i)] = q
            for b in range(LB // LANE):
                top = jnp.maximum(top, q[:, b * LANE:(b + 1) * LANE])
            return top

        top = lax.fori_loop(0, V // LB, seek, jnp.full((KC, LANE), -jnp.inf, jnp.float32))
        top = jnp.broadcast_to(jnp.max(top, axis=1, keepdims=True), (KC, LANE))
        tops = tiled(top)

        def block(i, sums):
            w = jnp.exp(base[krows(c), lanes(i)] - tops)
            base[krows(c), lanes(i)] = w
            return tuple(narrow(sums[t], w * work[c, t, :, lanes(i)]) for t in range(T))

        sums = lax.fori_loop(0, V // LB, block, tuple(jnp.zeros((KC, LANE), jnp.float32) for _ in range(T)))
        lane = lax.broadcasted_iota(jnp.int32, (KC, LANE), 1)
        packed = jnp.where(lane < 2 * T, known[c], top)
        for t in range(T):
            packed = jnp.where(lane == t, jnp.sum(sums[t], axis=1, keepdims=True), packed)
        stat[c] = jnp.where(lane[:HB] < LANE // 2, packed[:HB], pltpu.roll(packed[HB:], LANE // 2, 1))
        for d in range(1, nz):
            stat_copy(d, c).start()

    def slopes(c):
        send(stat_in.at[c], stat_in.at[c], stat_s.at[0], stat_r.at[c], {"tm": partner}).wait_recv()
        seen = [stat[c]] + [stat_in[c, d - 1] for d in range(1, nz)]
        tops = [pltpu.roll(x, LANE - 2 * T, 1) for x in seen]
        best, tokens = tops[0], seen[0]
        for d in range(1, nz):
            best = jnp.maximum(best, tops[d])
            tokens = tokens + seen[d]
        factor = [jnp.exp(top - best) for top in tops]
        total = factor[0] * seen[0]
        for d in range(1, nz):
            total = total + factor[d] * seen[d]
        r = factor[0] * pltpu.roll(tokens, LANE - T, 1) / total
        for t in range(T):
            for h in range(2):
                k = h * (LANE // 2) + t
                ratio[c, t, h * HB:(h + 1) * HB] = jnp.broadcast_to(r[:, k:k + 1], (HB, LANE))

        def block(i, _):
            drawn = jnp.zeros((KC, LB), jnp.float32)
            for t in range(T):
                drawn = drawn + tiled(ratio[c, t]) * work[c, t, :, lanes(i)]
            own[1, c, :, :, lanes(i)] = two(whole[c, :, lanes(i)] - base[krows(c), lanes(i)] * drawn)
            return 0

        lax.fori_loop(0, V // LB, block, 0)
        mate_copy(1, c).start()

    def finish(c):
        share_copy(1, c).wait_recv()
        sp = tiled(spread[c])

        def block(i, _):
            w = base[krows(c), lanes(i)]
            run = enter[1, c, :, :, lanes(i)].reshape(KC, LB)
            drawn = jnp.zeros((KC, LB), jnp.float32)
            for t in reversed(range(T)):
                drawn = drawn + tiled(ratio[c, t]) * work[c, t, :, lanes(i)]
                run = run + counts[t, krows(c), lanes(i)].astype(jnp.float32)
                value = sp * (run - w * drawn) - noise[c, t, :, lanes(i)].astype(jnp.float32)
                noise[c, t, :, lanes(i)] = value.astype(jnp.bfloat16)
            return 0

        lax.fori_loop(0, V // LB, block, 0)
        store_out(c).start()

    for k in range(EARLY):
        local(NC - 1 - k)
    load_counts.start()
    load_base.start()
    pl.semaphore_wait(barrier, nb + nz + jnp.where(chip == 0, n - 1, 0))
    for k in range(EARLY):
        mate_copy(0, NC - 1 - k).start()

    def opening(c):
        local(c)
        mate_copy(0, c).start()

    stages = [functools.partial(first, 0), functools.partial(hop, 0, 0), functools.partial(hop, 0, 1), soft, slopes,
              functools.partial(first, 1), functools.partial(hop, 1, 0), functools.partial(hop, 1, 1), finish, expand, opening]
    for st, k in ORDER:
        stages[st](NC - 1 - k)

    begin = me * rows - ((me * rows) // KC) * KC
    if per == 1:
        for h in range(2):
            @pl.when(me != h)
            def _():
                send(tot_out.at[0], tot.at[h], tot_s.at[0, 0], tot_r.at[h], {"tm": h}).wait_recv()
    else:
        @pl.when(me != begin // HB)
        def _():
            send(tot_out.at[0], tot.at[0], tot_s.at[0, 0], tot_r.at[0], {"tm": 0}).wait_recv()
    if per == 1:
        done = [pltpu.make_async_copy(tot.at[h], gb_hbm.at[pl.ds(h * HB, HB), :], gb_sem.at[h]) for h in range(2)]
    else:
        done = [pltpu.make_async_copy(tot.at[0], gb_hbm, gb_sem.at[0])]
    for copy in done:
        copy.start()

    def sent(ref, sem):
        send(ref, ref, sem, hop_r.at[0, 0, 0], {"tm": partner}).wait_send()

    for p in (0, 1):
        sent(mate.at[p], mate_s.at[p])
        sent(share.at[p], acc_s.at[p])
        for a in range(2):
            for j in range(nb):
                guarded(sends(p, a, j), lambda p=p, a=a, j=j: sent(src.at[p, j, :, :, half(a)], hop_s.at[p, a, j]))
    for d in range(1, nz):
        sent(stat, stat_s.at[d - 1])

    def drain(c):
        for e in range(per):
            @pl.when((chip == 0) & holds(e) & (owner(c, e) != me))
            def _():
                tot_copy(c, e).wait_send()

    each(drain)
    pltpu.make_async_copy(noise, gn_hbm, out_sem.at[0]).wait()
    for copy in done:
        copy.wait()


def place(parts, base, gn_hbm, gb_hbm, sem):
    NC = parts.shape[0]
    copies = [pltpu.make_async_copy(parts.at[c], gn_hbm.at[:, pl.ds(c * KC, KC), :], sem.at[c]) for c in range(NC)]
    copies.append(pltpu.make_async_copy(base, gb_hbm, sem.at[NC]))
    for copy in copies:
        copy.start()
    for copy in copies:
        copy.wait()


def per_device(n, nz, drift_noise, counts, base_logits, drift_scale):
    T, K, V = drift_noise.shape
    nb = n.bit_length() - 2
    rows = K // n
    out_rows = KC if rows >= KC else HB
    NC = K // KC
    f32, bf16 = jnp.float32, jnp.bfloat16
    dma = pltpu.SemaphoreType.DMA
    any_space = pl.BlockSpec(memory_space=pl.ANY)
    peers = max(nz - 1, 1)
    parts, grad_base = pl.pallas_call(
        functools.partial(kernel, n, nz, nb, rows, out_rows, (T, K, V)),
        out_shape=(jax.ShapeDtypeStruct((NC, T, KC, V), bf16), jax.ShapeDtypeStruct((out_rows, V), f32)),
        in_specs=[any_space] * 4,
        out_specs=(any_space, any_space),
        scratch_shapes=[
            pltpu.VMEM((NC, T, KC, V), bf16),
            pltpu.VMEM((T, K, V), bf16),
            pltpu.VMEM((K, V), f32),
            pltpu.VMEM((1, K), f32),
            pltpu.VMEM((NC, KC, LANE), f32),
            pltpu.VMEM((NC, T, KC, V), f32),
            pltpu.VMEM((NC, KC, V), f32),
            pltpu.VMEM((NC, T, KC, LANE), f32),
            pltpu.VMEM((NC, KC, LANE), f32),
            pltpu.VMEM((NC, HB, LANE), f32),
            pltpu.VMEM((NC, peers, HB, LANE), f32),
            pltpu.VMEM((2, HB, V), f32),
            pltpu.VMEM((NC, HB, V), f32),
            pltpu.VMEM((2, NC, 2, HB, V), f32),
            pltpu.VMEM((2, NC, HB, V), f32),
            pltpu.VMEM((2, nb, NC, HB, V), f32),
            pltpu.VMEM((2, nb, NC, HB, V), f32),
            pltpu.VMEM((2, NC, HB, V), f32),
            pltpu.VMEM((2, NC, HB, V), f32),
            pltpu.VMEM((2, NC, 2, HB, V), f32),
            dma((NC + 2,)), dma((1,)), dma((2,)), dma((1,)),
            dma((2,)), dma((NC,)),
            dma((2, 2, nb)), dma((2, nb, NC)),
            dma((2,)), dma((NC,)),
            dma((peers,)), dma((NC,)),
            dma((NC, KC // rows)), dma((2,)),
        ],
        compiler_params=pltpu.CompilerParams(
            collective_id=0, has_side_effects=True, vmem_limit_bytes=46 * 1024 * 1024),
    )(*[pltpu.with_memory_space_constraint(x, pltpu.HBM) for x in (drift_noise, counts, base_logits, drift_scale.reshape(1, K))])
    grad_noise, grad_base = pl.pallas_call(
        place,
        out_shape=(jax.ShapeDtypeStruct((T, K, V), bf16), jax.ShapeDtypeStruct((out_rows, V), f32)),
        in_specs=[any_space] * 2,
        out_specs=(any_space, any_space),
        scratch_shapes=[dma((NC + 1,))],
        compiler_params=pltpu.CompilerParams(vmem_limit_bytes=1024 * 1024),
    )(parts, grad_base)
    if rows < out_rows:
        start = lax.rem(lax.axis_index("tm") * rows, out_rows)
        grad_base = lax.dynamic_slice_in_dim(grad_base, start, rows, 0)
    return grad_noise, grad_base


def solution(mesh):
    n, nz = mesh.shape["tm"], mesh.shape["vocab"]
    return jax.shard_map(
        functools.partial(per_device, n, nz),
        mesh=mesh,
        in_specs=(P("tm", None, "vocab"), P("tm", None, "vocab"), P(None, "vocab"), P()),
        out_specs=(P("tm", None, "vocab"), P("tm", "vocab")),
        check_vma=False,
    )
```

```python
import functools

import jax
import jax.numpy as jnp
from jax import lax
from jax.experimental import pallas as pl
from jax.experimental.pallas import tpu as pltpu
from jax.sharding import PartitionSpec as P

MESH = pl.DeviceIdType.MESH
KC = 16
HB = KC // 2
LANE = 128
EARLY = 3
ORDER = [(10, 3), (0, 0), (10, 4), (0, 1), (10, 5), (0, 2), (10, 6), (0, 3), (10, 7), (9, 0), (9, 1), (9, 2), (0, 4), (9, 3), (1, 0), (0, 5), (9, 4), (1, 1), (0, 6), (9, 5), (1, 2), (0, 7), (9, 6), (9, 7), (1, 3), (1, 4), (2, 0), (1, 5), (2, 1), (3, 0), (1, 6), (2, 2), (3, 1), (1, 7), (2, 3), (3, 2), (2, 4), (3, 3), (2, 5), (3, 4), (2, 6), (4, 0), (3, 5), (2, 7), (4, 1), (3, 6), (5, 0), (4, 2), (3, 7), (5, 1), (4, 3), (5, 2), (4, 4), (5, 3), (4, 5), (5, 4), (4, 6), (5, 5), (4, 7), (6, 0), (5, 6), (6, 1), (5, 7), (6, 2), (6, 3), (6, 4), (6, 5), (7, 0), (6, 6), (7, 1), (6, 7), (7, 2), (8, 0), (7, 3), (8, 1), (7, 4), (8, 2), (7, 5), (8, 3), (7, 6), (8, 4), (7, 7), (8, 5), (8, 6), (8, 7)]


def kernel(n, nz, nb, rows, out_rows, dims,
           noise_hbm, counts_hbm, base_hbm, scale_hbm, gn_hbm, gb_hbm,
           noise, counts, base, scale_ref, spread, work, whole, ratio, known, stat, stat_in, tot, tot_out,
           own, mate, src, got, part, share, enter,
           in_sem, out_sem, gb_sem, scale_sem, mate_s, mate_r, hop_s, hop_r, acc_s, acc_r, stat_s, stat_r, tot_s, tot_r):
    T, K, V = dims
    NC = K // KC
    LB = min(512, V)
    VH = V // 2
    per = KC // rows
    me = lax.axis_index("tm")
    z = lax.axis_index("vocab")
    core = lax.rem(me, 2)
    partner = me + 1 - 2 * core
    chip = me // 2

    def bit(j):
        return lax.rem(chip // (2 ** j), 2)

    def across(j):
        return me + (1 - 2 * bit(j)) * (2 ** (j + 1))

    def order(a, j):
        return j if a == 0 else nb - 1 - j

    def upper(p, b):
        return bit(b) == 1 - p

    def above(p, b):
        high = chip // (2 ** (b + 1))
        return high != (0 if p == 0 else 2 ** (nb - 1 - b) - 1)

    def always(x):
        return isinstance(x, bool)

    def sends(p, a, j):
        b = order(a, j)
        if a == 0:
            return True if j < nb - 1 else jnp.logical_not(upper(p, b))
        low = jnp.logical_not(upper(p, b))
        return low if j == 0 else jnp.logical_or(low, above(p, b))

    def receives(p, a, j):
        b = order(a, j)
        if a == 0:
            return True if j < nb - 1 else upper(p, b)
        return upper(p, b) if j == 0 else jnp.logical_or(upper(p, b), above(p, b))

    def guarded(cond, fn):
        if always(cond):
            fn()
        else:
            pl.when(cond)(fn)

    def half(a):
        return pl.ds(a * VH, VH)

    def krows(c):
        return pl.ds(c * KC if isinstance(c, int) else pl.multiple_of(c * KC, KC), KC)

    def load_noise(c):
        return pltpu.make_async_copy(noise_hbm.at[:, krows(c), :], noise.at[c], in_sem.at[c])

    load_counts = pltpu.make_async_copy(counts_hbm, counts, in_sem.at[NC])
    load_base = pltpu.make_async_copy(base_hbm, base, in_sem.at[NC + 1])

    def store_out(c):
        return pltpu.make_async_copy(noise.at[c], gn_hbm.at[c], out_sem.at[0])

    def send(a, b, s, r, device):
        return pltpu.make_async_remote_copy(src_ref=a, dst_ref=b, send_sem=s, recv_sem=r,
                                            device_id=device, device_id_type=MESH)

    def mate_copy(p, c):
        return send(own.at[p, c, 1 - core], mate.at[p, c], mate_s.at[p], mate_r.at[c], {"tm": partner})

    def hop_copy(p, a, j, c):
        return send(src.at[p, j, c, :, half(a)], got.at[p, j, c, :, half(a)],
                    hop_s.at[p, a, j], hop_r.at[p, j, c], {"tm": across(order(a, j))})

    def share_copy(p, c):
        return send(share.at[p, c], enter.at[p, c, core], acc_s.at[p], acc_r.at[c], {"tm": partner})

    def stat_copy(d, c):
        return send(stat.at[c], stat_in.at[c, d - 1], stat_s.at[d - 1], stat_r.at[c],
                    {"vocab": lax.rem(z + d, nz)})

    def slot():
        return core if per == 1 else 0

    def owner(c, e):
        return c * per + e

    def tot_copy(c, e):
        return send(tot_out.at[c], tot.at[slot()], tot_s.at[c, e], tot_r.at[slot()], {"tm": owner(c, e)})

    def holds(e):
        return chip == 0 if per == 1 else me == (e * rows) // HB

    def each(fn):
        lax.fori_loop(0, NC, lambda i, _: (fn(NC - 1 - i), 0)[1], 0)

    barrier = pltpu.get_barrier_semaphore()
    for d in range(nz - 1, 0, -1):
        pl.semaphore_signal(barrier, inc=1, device_id={"vocab": lax.rem(z + d, nz)}, device_id_type=MESH)
    for h in range(2):
        @pl.when(me != h)
        def _():
            pl.semaphore_signal(barrier, inc=1, device_id={"tm": h}, device_id_type=MESH)
    pl.semaphore_signal(barrier, inc=1, device_id={"tm": partner}, device_id_type=MESH)
    for j in range(nb):
        pl.semaphore_signal(barrier, inc=1, device_id={"tm": across(j)}, device_id_type=MESH)

    load_scale = pltpu.make_async_copy(scale_hbm, scale_ref, scale_sem.at[0])
    load_scale.start()
    each(lambda c: load_noise(c).start())

    load_scale.wait()
    wide = jnp.broadcast_to(scale_ref[...], (LANE, LANE)).T
    for c in range(NC):
        spread[c] = wide[c * KC:(c + 1) * KC]

    def lanes(i):
        return pl.ds(pl.multiple_of(i * LB, LB), LB)

    def tiled(x):
        return jnp.concatenate([x] * (LB // LANE), axis=1)

    def two(x):
        return x.reshape(2, HB, x.shape[-1])

    def narrow(sums, e):
        for b in range(LB // LANE):
            sums = sums + e[:, b * LANE:(b + 1) * LANE]
        return sums

    def local(c):
        load_noise(c).wait()
        sp = tiled(spread[c])

        def block(i, _):
            total = jnp.zeros((KC, LB), jnp.float32)
            for t in range(T):
                total = total + noise[c, t, :, lanes(i)].astype(jnp.float32)
            own[0, c, :, :, lanes(i)] = two(sp * total)
            return 0

        lax.fori_loop(0, V // LB, block, 0)

    def expand(c):
        if c == NC - 1:
            load_counts.wait()
        sp = tiled(spread[c])

        def block(i, sums):
            total = jnp.zeros((KC, LB), jnp.float32)
            seen = jnp.zeros((KC, LB), jnp.float32)
            new = []
            for t in range(T):
                total = total + noise[c, t, :, lanes(i)].astype(jnp.float32)
                work[c, t, :, lanes(i)] = jnp.exp(sp * total)
                count = counts[t, krows(c), lanes(i)].astype(jnp.float32)
                seen = seen + count
                new.append(narrow(sums[t], count))
            whole[c, :, lanes(i)] = seen
            return tuple(new)

        sums = lax.fori_loop(0, V // LB, block, tuple(jnp.zeros((KC, LANE), jnp.float32) for _ in range(T)))
        lane = lax.broadcasted_iota(jnp.int32, (KC, LANE), 1)
        packed = jnp.zeros((KC, LANE), jnp.float32)
        for t in range(T):
            packed = jnp.where(lane == T + t, jnp.sum(sums[t], axis=1, keepdims=True), packed)
        known[c] = packed

    def start_hops(p, j, c):
        for a in ((0, 1) if (j + p) % 2 == 0 else (1, 0)):
            guarded(sends(p, a, j), lambda a=a: hop_copy(p, a, j, c).start())

    def first(p, c):
        mate_copy(p, c).wait_recv()
        src[p, 0, c] = own[p, c, core] + mate[p, c]
        part[p, c] = jnp.zeros((HB, V), jnp.float32)
        start_hops(p, 0, c)

    def hop(p, j, c):
        gets = [receives(p, a, j) for a in range(2)]
        if always(gets[0]):
            gets[0] = chip >= 0

        @pl.when(gets[0] & gets[1])
        def _():
            send(got.at[p, j, c], got.at[p, j, c], hop_s.at[p, 0, j], hop_r.at[p, j, c], {"tm": partner}).wait_recv()

        @pl.when(gets[0] != gets[1])
        def _():
            hop_copy(p, 0, j, c).wait_recv()

        for a in range(2):
            up = upper(p, order(a, j))

            def take(a=a, up=up):
                arrived = got[p, j, c, :, half(a)]
                if a == 0:
                    if j < nb - 1:
                        src[p, j + 1, c, :, half(a)] = src[p, j, c, :, half(a)] + arrived
                        arrived = jnp.where(up, arrived, jnp.zeros_like(arrived))
                part[p, c, :, half(a)] = part[p, c, :, half(a)] + arrived

            guarded(receives(p, a, j), take)
        if j < nb - 1:
            low = jnp.logical_not(upper(p, order(1, j + 1)))
            chips = src[p, 0, c, :, half(1)]
            src[p, j + 1, c, :, half(1)] = part[p, c, :, half(1)] + jnp.where(low, chips, jnp.zeros_like(chips))
            start_hops(p, j + 1, c)
            return
        before = part[p, c]
        leads = core == p
        mine, other = own[p, c, core], mate[p, c]
        zero = jnp.zeros_like(before)
        share[p, c] = before + jnp.where(leads, mine, zero)
        enter[p, c, core] = before + jnp.where(leads, zero, other)
        share_copy(p, c).start()
        if p == 1:
            @pl.when(chip == 0)
            def _():
                tot_out[c] = before + src[1, 0, c]
                for e in range(per):
                    @pl.when(holds(e) & (owner(c, e) != me))
                    def _():
                        tot_copy(c, e).start()

                    @pl.when(holds(e) & (owner(c, e) == me))
                    def _():
                        tot[slot()] = tot_out[c]

    def soft(c):
        share_copy(0, c).wait_recv()
        if c == NC - 1:
            load_base.wait()

        def seek(i, top):
            q = base[krows(c), lanes(i)] + enter[0, c, :, :, lanes(i)].reshape(KC, LB)
            base[krows(c), lanes(i)] = q
            for b in range(LB // LANE):
                top = jnp.maximum(top, q[:, b * LANE:(b + 1) * LANE])
            return top

        top = lax.fori_loop(0, V // LB, seek, jnp.full((KC, LANE), -jnp.inf, jnp.float32), unroll=min(2, V // LB))
        top = jnp.broadcast_to(jnp.max(top, axis=1, keepdims=True), (KC, LANE))
        tops = tiled(top)

        def block(i, sums):
            w = jnp.exp(base[krows(c), lanes(i)] - tops)
            base[krows(c), lanes(i)] = w
            return tuple(narrow(sums[t], w * work[c, t, :, lanes(i)]) for t in range(T))

        sums = lax.fori_loop(0, V // LB, block, tuple(jnp.zeros((KC, LANE), jnp.float32) for _ in range(T)))
        lane = lax.broadcasted_iota(jnp.int32, (KC, LANE), 1)
        packed = jnp.where(lane < 2 * T, known[c], top)
        for t in range(T):
            packed = jnp.where(lane == t, jnp.sum(sums[t], axis=1, keepdims=True), packed)
        stat[c] = jnp.where(lane[:HB] < LANE // 2, packed[:HB], pltpu.roll(packed[HB:], LANE // 2, 1))
        for d in range(1, nz):
            stat_copy(d, c).start()

    def slopes(c):
        send(stat_in.at[c], stat_in.at[c], stat_s.at[0], stat_r.at[c], {"tm": partner}).wait_recv()
        seen = [stat[c]] + [stat_in[c, d - 1] for d in range(1, nz)]
        tops = [pltpu.roll(x, LANE - 2 * T, 1) for x in seen]
        best, tokens = tops[0], seen[0]
        for d in range(1, nz):
            best = jnp.maximum(best, tops[d])
            tokens = tokens + seen[d]
        factor = [jnp.exp(top - best) for top in tops]
        total = factor[0] * seen[0]
        for d in range(1, nz):
            total = total + factor[d] * seen[d]
        r = factor[0] * pltpu.roll(tokens, LANE - T, 1) / total
        for t in range(T):
            for h in range(2):
                k = h * (LANE // 2) + t
                ratio[c, t, h * HB:(h + 1) * HB] = jnp.broadcast_to(r[:, k:k + 1], (HB, LANE))

        def block(i, _):
            drawn = jnp.zeros((KC, LB), jnp.float32)
            for t in range(T):
                drawn = drawn + tiled(ratio[c, t]) * work[c, t, :, lanes(i)]
            own[1, c, :, :, lanes(i)] = two(whole[c, :, lanes(i)] - base[krows(c), lanes(i)] * drawn)
            return 0

        lax.fori_loop(0, V // LB, block, 0, unroll=min(2, V // LB))
        mate_copy(1, c).start()

    def finish(c):
        share_copy(1, c).wait_recv()
        sp = tiled(spread[c])

        def block(i, _):
            w = base[krows(c), lanes(i)]
            run = enter[1, c, :, :, lanes(i)].reshape(KC, LB)
            drawn = jnp.zeros((KC, LB), jnp.float32)
            for t in reversed(range(T)):
                drawn = drawn + tiled(ratio[c, t]) * work[c, t, :, lanes(i)]
                run = run + counts[t, krows(c), lanes(i)].astype(jnp.float32)
                value = sp * (run - w * drawn) - noise[c, t, :, lanes(i)].astype(jnp.float32)
                noise[c, t, :, lanes(i)] = value.astype(jnp.bfloat16)
            return 0

        lax.fori_loop(0, V // LB, block, 0)
        store_out(c).start()

    for k in range(EARLY):
        local(NC - 1 - k)
    load_counts.start()
    load_base.start()
    pl.semaphore_wait(barrier, nb + nz + jnp.where(chip == 0, n - 1, 0))
    for k in range(EARLY):
        mate_copy(0, NC - 1 - k).start()

    def opening(c):
        local(c)
        mate_copy(0, c).start()

    stages = [functools.partial(first, 0), functools.partial(hop, 0, 0), functools.partial(hop, 0, 1), soft, slopes,
              functools.partial(first, 1), functools.partial(hop, 1, 0), functools.partial(hop, 1, 1), finish, expand, opening]
    for st, k in ORDER:
        stages[st](NC - 1 - k)

    begin = me * rows - ((me * rows) // KC) * KC
    if per == 1:
        for h in range(2):
            @pl.when(me != h)
            def _():
                send(tot_out.at[0], tot.at[h], tot_s.at[0, 0], tot_r.at[h], {"tm": h}).wait_recv()
    else:
        @pl.when(me != begin // HB)
        def _():
            send(tot_out.at[0], tot.at[0], tot_s.at[0, 0], tot_r.at[0], {"tm": 0}).wait_recv()
    if per == 1:
        done = [pltpu.make_async_copy(tot.at[h], gb_hbm.at[pl.ds(h * HB, HB), :], gb_sem.at[h]) for h in range(2)]
    else:
        done = [pltpu.make_async_copy(tot.at[0], gb_hbm, gb_sem.at[0])]
    for copy in done:
        copy.start()

    def sent(ref, sem):
        send(ref, ref, sem, hop_r.at[0, 0, 0], {"tm": partner}).wait_send()

    for p in (0, 1):
        sent(mate.at[p], mate_s.at[p])
        sent(share.at[p], acc_s.at[p])
        for a in range(2):
            for j in range(nb):
                guarded(sends(p, a, j), lambda p=p, a=a, j=j: sent(src.at[p, j, :, :, half(a)], hop_s.at[p, a, j]))
    for d in range(1, nz):
        sent(stat, stat_s.at[d - 1])

    def drain(c):
        for e in range(per):
            @pl.when((chip == 0) & holds(e) & (owner(c, e) != me))
            def _():
                tot_copy(c, e).wait_send()

    each(drain)
    pltpu.make_async_copy(noise, gn_hbm, out_sem.at[0]).wait()
    for copy in done:
        copy.wait()


def place(parts, base, gn_hbm, gb_hbm, sem):
    NC = parts.shape[0]
    copies = [pltpu.make_async_copy(parts.at[c], gn_hbm.at[:, pl.ds(c * KC, KC), :], sem.at[c]) for c in range(NC)]
    copies.append(pltpu.make_async_copy(base, gb_hbm, sem.at[NC]))
    for copy in copies:
        copy.start()
    for copy in copies:
        copy.wait()


def per_device(n, nz, drift_noise, counts, base_logits, drift_scale):
    T, K, V = drift_noise.shape
    nb = n.bit_length() - 2
    rows = K // n
    out_rows = KC if rows >= KC else HB
    NC = K // KC
    f32, bf16 = jnp.float32, jnp.bfloat16
    dma = pltpu.SemaphoreType.DMA
    any_space = pl.BlockSpec(memory_space=pl.ANY)
    peers = max(nz - 1, 1)
    parts, grad_base = pl.pallas_call(
        functools.partial(kernel, n, nz, nb, rows, out_rows, (T, K, V)),
        out_shape=(jax.ShapeDtypeStruct((NC, T, KC, V), bf16), jax.ShapeDtypeStruct((out_rows, V), f32)),
        in_specs=[any_space] * 4,
        out_specs=(any_space, any_space),
        scratch_shapes=[
            pltpu.VMEM((NC, T, KC, V), bf16),
            pltpu.VMEM((T, K, V), bf16),
            pltpu.VMEM((K, V), f32),
            pltpu.VMEM((1, K), f32),
            pltpu.VMEM((NC, KC, LANE), f32),
            pltpu.VMEM((NC, T, KC, V), f32),
            pltpu.VMEM((NC, KC, V), f32),
            pltpu.VMEM((NC, T, KC, LANE), f32),
            pltpu.VMEM((NC, KC, LANE), f32),
            pltpu.VMEM((NC, HB, LANE), f32),
            pltpu.VMEM((NC, peers, HB, LANE), f32),
            pltpu.VMEM((2, HB, V), f32),
            pltpu.VMEM((NC, HB, V), f32),
            pltpu.VMEM((2, NC, 2, HB, V), f32),
            pltpu.VMEM((2, NC, HB, V), f32),
            pltpu.VMEM((2, nb, NC, HB, V), f32),
            pltpu.VMEM((2, nb, NC, HB, V), f32),
            pltpu.VMEM((2, NC, HB, V), f32),
            pltpu.VMEM((2, NC, HB, V), f32),
            pltpu.VMEM((2, NC, 2, HB, V), f32),
            dma((NC + 2,)), dma((1,)), dma((2,)), dma((1,)),
            dma((2,)), dma((NC,)),
            dma((2, 2, nb)), dma((2, nb, NC)),
            dma((2,)), dma((NC,)),
            dma((peers,)), dma((NC,)),
            dma((NC, KC // rows)), dma((2,)),
        ],
        compiler_params=pltpu.CompilerParams(
            collective_id=0, has_side_effects=True, vmem_limit_bytes=46 * 1024 * 1024),
    )(*[pltpu.with_memory_space_constraint(x, pltpu.HBM) for x in (drift_noise, counts, base_logits, drift_scale.reshape(1, K))])
    grad_noise, grad_base = pl.pallas_call(
        place,
        out_shape=(jax.ShapeDtypeStruct((T, K, V), bf16), jax.ShapeDtypeStruct((out_rows, V), f32)),
        in_specs=[any_space] * 2,
        out_specs=(any_space, any_space),
        scratch_shapes=[dma((NC + 1,))],
        compiler_params=pltpu.CompilerParams(vmem_limit_bytes=1024 * 1024),
    )(parts, grad_base)
    if rows < out_rows:
        start = lax.rem(lax.axis_index("tm") * rows, out_rows)
        grad_base = lax.dynamic_slice_in_dim(grad_base, start, rows, 0)
    return grad_noise, grad_base


def solution(mesh):
    n, nz = mesh.shape["tm"], mesh.shape["vocab"]
    return jax.shard_map(
        functools.partial(per_device, n, nz),
        mesh=mesh,
        in_specs=(P("tm", None, "vocab"), P("tm", None, "vocab"), P(None, "vocab"), P()),
        out_specs=(P("tm", None, "vocab"), P("tm", "vocab")),
        check_vma=False,
    )
```
